32 devices in a mesh: gx: 4 (over y, core), gy: 8 (over z, x).
Axes of the slice: x: 2, y: 2, z: 4, core: 2. Of those that a mesh axis runs over, the one named last changes fastest.
Arguments:
- velocity: float32 [3, 32, 64, 128], P(None, 'gx', 'gy'), may hold values from -2 to 2
- pressure: float32 [32, 64, 128], P('gx', 'gy'), may hold values from -6 to 6
- buoyancy: float32 [32, 64, 128], P('gx', 'gy'), may hold values from -6 to 6
- background: float32 [32, 64, 128], P('gx', 'gy'), may hold values from -0.7 to 0.7
- marker_value: float32 [8192, 256], P(('gx', 'gy')), may hold values from -2.5 to 2.5
- marker_height: float32 [8192, 256], P(('gx', 'gy')), may hold values from 0 to 127
- marker_owner: int32 [8192, 1], P(('gx', 'gy')), may hold values from 0 to 31; in each aligned block of 256 rows (0 to 255, 256 to 511, ...) at most 16 rows name the same one
- marker_column: int32 [8192], P(('gx', 'gy')), may hold values from 0 to 63
- block_count: int32 [32], P(('gx', 'gy')), may hold values from 1 to 256, 6144 in all
Outputs:
- new_velocity: float32 [3, 32, 64, 128], P(None, 'gx', 'gy')
- new_pressure: float32 [32, 64, 128], P('gx', 'gy')
- viscosity: float32 [32, 64, 128], P('gx', 'gy')
The draws below stay inside these ranges and needn't reach their ends.
Inputs may be any that keep to these rules, and one draw needn't show every extreme that they name: `marker_owner`: among the 256 blocks of one device at most 16 name the same owner, and for some owner exactly 16 do. A device's live blocks are its first block_count ones; some device has all 256 live.
All inputs are finite; a program needn't handle non-finite values.
Results may differ from the reference program's by a relative error of at most 0.0003.
Values sent between devices are 32-bit elements; how exact they have to be, the bound alone decides.
No kernel may reach another device: no remote copies, remote signals or barrier semaphores. Data moves between devices by JAX's collectives and lax.ppermute only.
A program may use at most 64 MiB of HBM per device.

```python
import math
import jax
import jax.numpy as jnp
import numpy as np

CX = 8
CY = 8
NZ = 128
MARK = 256
BLK_DEV = 256
ITERS = 2
CAP = 16
NX = 32
NY = 64
BLOCKS = 8192
N_GX = 4
N_GY = 8


def plant(values, stream_key, low, largest):
    dims = values.shape
    index_at = [jax.random.randint(jax.random.fold_in(stream_key, axis), (), 0, dims[axis]) for axis in range(len(dims))]
    values = values.at[tuple(index_at)].set(low)
    longest = dims.index(max(dims))
    index_at[longest] = (index_at[longest] + 1) % dims[longest]
    return values.at[tuple(index_at)].set(largest)


def levels(stream_key, extent, split, low, top_value):
    factor_of, own = 1.0, jax.random.fold_in(stream_key, 6)
    for dim, blocks in split:
        steps = jnp.exp(jax.random.uniform(jax.random.fold_in(own, dim), (blocks,), jnp.float32, low / len(split), top_value / len(split)))
        factor_of = factor_of * jnp.repeat(steps, extent[dim] // blocks).reshape([-1 if axis == dim else 1 for axis in range(len(extent))])
    return factor_of


def length_profile(count, total, bound, slope):
    weights = [(1 << 20) // math.isqrt(grade ** slope) + 1 for grade in range(2, count + 1)]
    surplus, holding = total - bound - (count - 1), [1] * (count - 1)
    while surplus > 0:
        free = [i for i in range(count - 1) if holding[i] < bound]
        pool, left = sum([weights[i] for i in free]), surplus
        for i in free:
            addition = min(bound - holding[i], max(1, left * weights[i] // pool), surplus)
            holding[i] = holding[i] + addition
            surplus = surplus - addition
    return np.array([bound] + holding)


def ragged(stream_key, count, total, reach, slope):
    if count == 2:
        one = jax.random.randint(stream_key, (), max(1, total - reach), min(reach, total - 1) + 1)
        return jnp.stack([one, total - one])
    sizes = jnp.asarray(length_profile(count, total, reach, slope), jnp.int32)
    couples = (count - 1) // 2
    source_of, sink = sizes[1:1 + 2 * couples:2], sizes[2:2 + 2 * couples:2]
    slack = jnp.minimum(source_of - 1, reach - sink)
    passed = jax.random.randint(jax.random.fold_in(stream_key, 1), (couples,), 0, 1 << 20) % (slack + 1)
    sizes = sizes.at[1:1 + 2 * couples:2].set(source_of - passed).at[2:2 + 2 * couples:2].set(sink + passed)
    return sizes[jax.random.permutation(jax.random.fold_in(stream_key, 2), count)]


def routed_block(key, own, number, rows, amount, top, reach, lean):
    order = jax.random.permutation(key, amount)
    heavy_load, usual = portions_of(amount, rows * top, reach, lean, True), portions_of(amount, rows * top, reach, lean, False)
    places = jnp.arange(amount)

    def named(sizes, offset_by):
        used = int((sizes > 0).sum())
        fixed = max(1, used // 4)
        shifted = fixed + (places - fixed + offset_by * (used - fixed)) % max(1, amount - fixed)
        return jnp.zeros((amount,), jnp.int32).at[order[jnp.where(places < fixed, places, shifted)]].set(jnp.asarray(sizes, jnp.int32))

    sizes = jnp.where(number % 4 == 0, named(heavy_load, number // 4), named(usual, number - number // 4 - 1))
    mixed = jax.random.permutation(jax.random.fold_in(own, 3), amount)
    source_of, receiver = mixed[0:amount // 2 * 2:2], mixed[1:amount // 2 * 2:2]
    margin = jnp.minimum(sizes[source_of] - 1, reach - sizes[receiver]) // 2
    margin = jnp.where((source_of == order[0]) | (receiver == order[0]) | (sizes[receiver] == 0), 0, jnp.maximum(margin, 0))
    shifted = jax.random.randint(jax.random.fold_in(own, 4), (amount // 2,), 0, 1 << 20) % (margin + 1)
    sizes = sizes.at[source_of].add(-shifted).at[receiver].add(shifted)
    items = jnp.searchsorted(jnp.cumsum(sizes), jnp.arange(rows * top), side="right").astype(jnp.int32)
    listing = items.reshape(top, rows).T
    listing = listing[jax.random.permutation(jax.random.fold_in(own, 1), rows)]
    offset_by = jax.random.randint(jax.random.fold_in(own, 2), (rows, 1), 0, top)
    return jnp.take_along_axis(listing, (jnp.arange(top)[None, :] + offset_by) % top, axis=1)


def portions_of(amount, total, most, lean, full):
    portions = [(1 << 20) // math.isqrt(grade ** lean) + 1 for grade in range(1, amount + 1)]
    largest = most if full else min(most, max(-(-total // amount), total * portions[0] // sum(portions)))
    least = 1 if total - largest >= amount - 1 else 0
    holding, spare = [largest] + [least] * (amount - 1), total - largest - least * (amount - 1)
    while spare > 0:
        candidates = [i for i in range(1, amount) if holding[i] < largest] or [i for i in range(1, amount) if holding[i] < most]
        mass, left = sum([portions[i] for i in candidates]), spare
        for i in candidates:
            addition = min(most - holding[i], max(1, left * portions[i] // mass), spare)
            holding[i] = holding[i] + addition
            spare = spare - addition
    return np.array(holding)


def noise(own_key, dims, scale, reach, shards=(), kind=jnp.bfloat16):
    drawn = jax.random.normal(own_key, dims, jnp.float32) * scale
    if len(shards) > 0:
        drawn = levels(own_key, dims, shards, -0.22, 0.18) * drawn
    return jnp.clip(drawn, min=-reach, max=reach).astype(kind)


def setup_inputs(seed: int = 0) -> dict:
    key_list = jax.random.split(jax.random.key(seed), 10)
    velocity = noise(key_list[0], (3, NX, NY, NZ), 0.3, 2.0, ((1, 4), (2, 8)), jnp.float32)
    pressure = noise(key_list[1], (NX, NY, NZ), 1.0, 6.0, ((0, 4), (1, 8)), jnp.float32)
    buoyancy = noise(key_list[2], (NX, NY, NZ), 1.0, 6.0, ((0, 4), (1, 8)), jnp.float32)
    background = jnp.clip(jax.random.uniform(key_list[3], (NX, NY, NZ), jnp.float32, -0.7, 0.7) * levels(key_list[3], (NX, NY, NZ), ((0, 4), (1, 8)), -0.4, 0.0), -0.7, 0.7)
    marker_value = noise(key_list[4], (BLOCKS, MARK), 0.7, 2.5, ((0, 32),), jnp.float32)
    marker_height = jnp.clip(127.0 * jax.random.uniform(key_list[5], (BLOCKS, MARK), jnp.float32) ** levels(key_list[5], (BLOCKS, MARK), ((0, 32),), -0.2, 0.2), 0.0, 127.0)
    marker_owner_keys = jax.random.split(jax.random.fold_in(key_list[6], 1), BLOCKS // BLK_DEV)
    marker_owner_turns = jax.random.permutation(jax.random.fold_in(key_list[6], 3), BLOCKS // BLK_DEV)
    marker_owner = jax.vmap(lambda own, number: routed_block(jax.random.fold_in(key_list[6], 2), own, number, BLK_DEV, N_GX * N_GY, 1, CAP, 2))(marker_owner_keys, marker_owner_turns).reshape((BLOCKS, 1))
    marker_column = plant(jax.random.randint(key_list[7], (BLOCKS,), 0, CX * CY), jax.random.fold_in(key_list[7], 1), 0, (CX * CY) - 1).astype(jnp.int32)
    block_count = ragged(key_list[8], N_GX * N_GY, 3 * BLK_DEV * N_GX * N_GY // 4, BLK_DEV, 2).astype(jnp.int32)
    return {"velocity": velocity, "pressure": pressure, "buoyancy": buoyancy, "background": background, "marker_value": marker_value, "marker_height": marker_height, "marker_owner": marker_owner, "marker_column": marker_column, "block_count": block_count}


PRESS_STEP = 0.5
VEL_STEP = 0.05
DAMPING = 0.8


def inner_of(field):
    return field[..., 1:-1, 1:-1, :]


def east_of(field):
    return field[..., 2:, 1:-1, :]


def west_of(field):
    return field[..., :-2, 1:-1, :]


def north_of(field):
    return field[..., 1:-1, 2:, :]


def south_of(field):
    return field[..., 1:-1, :-2, :]


def upper_of(field):
    return jnp.concatenate([field[..., 1:], jnp.zeros_like(field[..., :1])], axis=-1)


def lower_of(field):
    return jnp.concatenate([jnp.zeros_like(field[..., :1]), field[..., :-1]], axis=-1)


def deposit(values, heights, rows, total_rows, num_levels):
    lower_f = jnp.minimum(jnp.floor(heights), num_levels - 2.0)
    fraction = heights - lower_f
    lower_idx = lower_f.astype(jnp.int32)
    row_idx = jnp.broadcast_to(rows[:, None], heights.shape).astype(jnp.int32)
    sums = jnp.zeros((total_rows + 1, 2, num_levels), jnp.float32)
    sums = sums.at[row_idx, 0, lower_idx].add(values * (1.0 - fraction))
    sums = sums.at[row_idx, 0, lower_idx + 1].add(values * fraction)
    sums = sums.at[row_idx, 1, lower_idx].add(1.0 - fraction)
    sums = sums.at[row_idx, 1, lower_idx + 1].add(fraction)
    return sums[:total_rows]


def stresses(vel_pad, visc_pad, pressure):
    vel_x = inner_of(vel_pad[0])
    vel_y = inner_of(vel_pad[1])
    vel_z = inner_of(vel_pad[2])
    visc = inner_of(visc_pad)
    grad_xx = vel_x - west_of(vel_pad[0])
    grad_yy = vel_y - south_of(vel_pad[1])
    grad_zz = vel_z - lower_of(vel_z)
    divergence = grad_xx + grad_yy + grad_zz
    new_press = pressure - PRESS_STEP * visc * divergence
    third = divergence / 3.0
    sig_xx = 2.0 * visc * (grad_xx - third) - new_press
    sig_yy = 2.0 * visc * (grad_yy - third) - new_press
    sig_zz = 2.0 * visc * (grad_zz - third) - new_press
    corner_xy = 0.25 * (visc + east_of(visc_pad) + north_of(visc_pad) + visc_pad[..., 2:, 2:, :])
    side_x = visc + east_of(visc_pad)
    side_y = visc + north_of(visc_pad)
    corner_xz = 0.25 * (side_x + upper_of(side_x))
    corner_yz = 0.25 * (side_y + upper_of(side_y))
    tau_xy = corner_xy * (north_of(vel_pad[0]) - vel_x + east_of(vel_pad[1]) - vel_y)
    tau_xz = corner_xz * (upper_of(vel_x) - vel_x + east_of(vel_pad[2]) - vel_z)
    tau_yz = corner_yz * (upper_of(vel_y) - vel_y + north_of(vel_pad[2]) - vel_z)
    return new_press, jnp.stack([sig_xx, sig_yy, tau_xy, tau_xz, tau_yz]), sig_zz


def residuals(stress_pad, sig_zz, buoyancy):
    sig_xx = stress_pad[0]
    sig_yy = stress_pad[1]
    tau_xy = stress_pad[2]
    tau_xz = stress_pad[3]
    tau_yz = stress_pad[4]
    mid_xz = inner_of(tau_xz)
    mid_yz = inner_of(tau_yz)
    res_x = east_of(sig_xx) - inner_of(sig_xx) + inner_of(tau_xy) - south_of(tau_xy) + mid_xz - lower_of(mid_xz)
    res_y = inner_of(tau_xy) - west_of(tau_xy) + north_of(sig_yy) - inner_of(sig_yy) + mid_yz - lower_of(mid_yz)
    res_z = mid_xz - west_of(tau_xz) + mid_yz - south_of(tau_yz) + upper_of(sig_zz) - sig_zz + buoyancy
    return jnp.stack([res_x, res_y, res_z])


def advance(vel, moment, residual, visc_pad, masks):
    visc = inner_of(visc_pad)
    faces = jnp.stack([0.5 * (visc + east_of(visc_pad)), 0.5 * (visc + north_of(visc_pad)), 0.5 * (visc + upper_of(visc))])
    moment = DAMPING * moment + residual
    vel = masks * (vel + VEL_STEP * moment / faces)
    return vel, moment


def pad_plane(field):
    widths = [(0, 0)] * (field.ndim - 3) + [(1, 1), (1, 1), (0, 0)]
    return jnp.pad(field, widths)


def reference(velocity, pressure, buoyancy, background, marker_value, marker_height, marker_owner, marker_column, block_count):
    order = jnp.arange(BLOCKS, dtype=jnp.int32)
    source = order // BLK_DEV
    live = (order % BLK_DEV) < block_count[source]
    owner = marker_owner[:, 0]
    per_row = NY // CY
    pos_x = (owner // per_row) * CX + marker_column // CY
    pos_y = (owner % per_row) * CY + marker_column % CY
    rows = jnp.where(live, pos_x * NY + pos_y, NX * NY).astype(jnp.int32)
    sums = deposit(marker_value, marker_height, rows, NX * NY, NZ).reshape(NX, NY, 2, NZ)
    viscosity = jnp.exp((sums[:, :, 0] + background) / (sums[:, :, 1] + 1.0))
    ones_grid = jnp.ones((NX, NY, NZ), jnp.float32)
    mask_x = (jnp.arange(NX) < NX - 1).astype(jnp.float32)
    mask_y = (jnp.arange(NY) < NY - 1).astype(jnp.float32)
    mask_z = (jnp.arange(NZ) < NZ - 1).astype(jnp.float32)
    masks = jnp.stack([ones_grid * mask_x[:, None, None], ones_grid * mask_y[None, :, None], ones_grid * mask_z[None, None, :]])
    visc_pad = pad_plane(viscosity)
    vel = velocity
    press = pressure
    moment = jnp.zeros_like(velocity)
    for sweep_idx in range(ITERS):
        press, stress, sig_zz = stresses(pad_plane(vel), visc_pad, press)
        residual = residuals(pad_plane(stress), sig_zz, buoyancy)
        vel, moment = advance(vel, moment, residual, visc_pad, masks)
    return vel, press, viscosity
```

```python
import functools

import jax
import jax.numpy as jnp
from jax import lax
from jax.experimental import pallas as pl
from jax.experimental.pallas import tpu as pltpu
from jax.sharding import PartitionSpec as P

ITERS = 2
HALO = 2

PRESS_STEP = 0.5
VEL_STEP = 0.05
DAMPING = 0.8

F32 = jnp.float32
BF16 = jnp.bfloat16
VMEM = pl.BlockSpec(memory_space=pltpu.VMEM)
SMEM = pl.BlockSpec(memory_space=pltpu.SMEM)
NT = (((1,), (1,)), ((), ()))
TN = (((0,), (0,)), ((), ()))


def split3(x):
    high = x.astype(BF16)
    rest = x - high.astype(F32)
    mid = rest.astype(BF16)
    low = (rest - mid.astype(F32)).astype(BF16)
    return high, mid, low


def deposit_kernel(
    num_owners, capacity, count_ref, owner_ref, column_ref, value_ref, height_ref, out_ref, part_ref
):
    blocks, marks = value_ref.shape
    num_levels = out_ref.shape[1] // 2
    row8 = lax.broadcasted_iota(jnp.int32, (8, marks), 0)
    upper_part = (row8 & 1) == 1
    with_value = (row8 & 2) == 0
    leading = row8 < 4
    level = lax.broadcasted_iota(jnp.int32, (num_levels, marks), 0).astype(F32).astype(BF16)

    def one_block(b):
        height = jnp.broadcast_to(height_ref[pl.ds(b, 1), :], (8, marks))
        value = jnp.broadcast_to(value_ref[pl.ds(b, 1), :], (8, marks))
        lower = jnp.minimum(jnp.floor(height), num_levels - 2.0)
        fraction = height - lower
        share = jnp.where(upper_part, fraction, 1.0 - fraction)
        share = share * jnp.where(with_value, value, 1.0)
        high = share.astype(BF16).astype(F32)
        pieces = jnp.where(leading, high, share - high)
        pieces = jnp.concatenate([pieces, pieces], axis=0).astype(BF16)
        lower16 = jnp.concatenate([lower, lower], axis=0).astype(BF16)
        lower_all = jnp.concatenate([lower16] * (num_levels // 16), axis=0)
        hot = jnp.where(lower_all == level, jnp.ones((), BF16), jnp.zeros((), BF16))
        sums = lax.dot_general(pieces, hot, NT, preferred_element_type=F32)
        part_ref[pl.ds(pl.multiple_of(b * 8, 8), 8), :] = sums[:8]

    def some_blocks(step, carry):
        for k in range(8):
            one_block(step * 8 + k)
        return carry

    lax.fori_loop(0, blocks // 8, some_blocks, 0)

    def part(kind):
        high = part_ref[pl.ds(kind, blocks, stride=8), :]
        return high + part_ref[pl.ds(kind + 4, blocks, stride=8), :]

    value_sum = part(0) + pltpu.roll(part(1), 1, 1)
    weight_sum = part(2) + pltpu.roll(part(3), 1, 1)

    owner = owner_ref[...]
    block_id = lax.broadcasted_iota(jnp.int32, (1, blocks), 1)
    owner = jnp.where(block_id < count_ref[0], owner, num_owners)
    owned = lax.broadcasted_iota(jnp.int32, (num_owners, blocks), 0) == owner
    hits = jnp.where(owned, 1.0, 0.0)
    earlier = jnp.where(
        lax.broadcasted_iota(jnp.int32, (blocks, blocks), 0)
        < lax.broadcasted_iota(jnp.int32, (blocks, blocks), 1),
        1.0,
        0.0,
    ).astype(BF16)
    before = jnp.dot(hits.astype(BF16), earlier, preferred_element_type=F32)
    rank = jnp.sum(hits * before, axis=0, keepdims=True)
    slot = owner * capacity + rank.astype(jnp.int32)
    slots = num_owners * capacity
    place = jnp.where(
        lax.broadcasted_iota(jnp.int32, (slots, blocks), 0) == slot, 1.0, 0.0
    ).astype(BF16)
    code = jnp.broadcast_to((column_ref[...] + 1).astype(F32), (num_levels, blocks)).astype(BF16)
    codes = lax.dot_general(place, code, NT, preferred_element_type=F32)

    def placed(x):
        high, mid, low = (jnp.dot(place, y, preferred_element_type=F32) for y in split3(x))
        return high + (mid + low)

    out_ref[:, :num_levels] = placed(value_sum)
    lane = lax.broadcasted_iota(jnp.int32, (slots, num_levels), 1)
    out_ref[:, num_levels:] = jnp.where(lane == num_levels - 1, codes, placed(weight_sum))


def deposit(count, owner, column, value, height, num_owners, capacity, num_levels):
    blocks, marks = value.shape
    return pl.pallas_call(
        functools.partial(deposit_kernel, num_owners, capacity),
        out_shape=jax.ShapeDtypeStruct((num_owners * capacity, 2 * num_levels), F32),
        in_specs=[SMEM, VMEM, VMEM, VMEM, VMEM],
        out_specs=VMEM,
        scratch_shapes=[pltpu.VMEM((blocks * 8, num_levels), F32)],
        compiler_params=pltpu.CompilerParams(vmem_limit_bytes=48 << 20),
        name="deposit",
    )(count, owner.reshape(1, blocks), column.reshape(1, blocks), value, height)


def gather_kernel(marks, arrived_ref, background_ref, out_ref):
    slots = arrived_ref.shape[0]
    columns, num_levels = out_ref.shape
    values = arrived_ref[:, :num_levels]
    weights = arrived_ref[:, num_levels:]
    lane = lax.broadcasted_iota(jnp.int32, (slots, num_levels), 1)
    last = lane == num_levels - 1
    code = weights[:, num_levels - 1 :]
    others = jnp.sum(jnp.where(last, 0.0, weights), axis=1, keepdims=True)
    weights = jnp.where(last, float(marks) - others, weights)
    place = jnp.where(code == (lane + 1).astype(F32), 1.0, 0.0).astype(BF16)

    def placed(x):
        high, mid, low = (
            lax.dot_general(place, y, TN, preferred_element_type=F32)[:columns] for y in split3(x)
        )
        return high + (mid + low)

    out_ref[...] = jnp.exp((placed(values) + background_ref[...]) / (placed(weights) + 1.0))


def gather(arrived, background, marks):
    cells_x, cells_y, num_levels = background.shape
    out = pl.pallas_call(
        functools.partial(gather_kernel, marks),
        out_shape=jax.ShapeDtypeStruct((cells_x * cells_y, num_levels), F32),
        in_specs=[VMEM, VMEM],
        out_specs=VMEM,
        compiler_params=pltpu.CompilerParams(vmem_limit_bytes=48 << 20),
        name="gather",
    )(arrived, background.reshape(cells_x * cells_y, num_levels))
    return out.reshape(cells_x, cells_y, num_levels)


def stokes_kernel(
    cells_y,
    limits_ref,
    vel_ref,
    press_ref,
    buoy_ref,
    visc_ref,
    new_vel_ref,
    new_press_ref,
):
    wide_x, rows, num_levels = visc_ref.shape
    cells_x = wide_x - 2 * HALO
    row = lax.broadcasted_iota(jnp.int32, (rows, num_levels), 0)
    lane = lax.broadcasted_iota(jnp.int32, (rows, num_levels), 1)
    first_x, size_x, first_y, size_y = (limits_ref[k] for k in range(4))
    at_y = row + (first_y - HALO)
    in_y = (at_y >= 0) & (at_y < size_y)
    in_y_face = (at_y >= 0) & (at_y < size_y - 1)
    low_lane = lane == 0
    high_lane = lane == num_levels - 1

    def north(f):
        return pltpu.roll(f, rows - 1, 0)

    def south(f):
        return pltpu.roll(f, 1, 0)

    def upper(f):
        return jnp.where(high_lane, 0.0, pltpu.roll(f, num_levels - 1, 1))

    def lower(f):
        return jnp.where(low_lane, 0.0, pltpu.roll(f, 1, 1))

    def in_x(x):
        at_x = first_x - HALO + x
        return (at_x >= 0) & (at_x < size_x)

    def in_x_face(x):
        at_x = first_x - HALO + x
        return (at_x >= 0) & (at_x < size_x - 1)

    visc = [visc_ref[x] for x in range(wide_x)]
    vel = [[vel_ref[c, x] for x in range(wide_x)] for c in range(3)]
    press = [press_ref[x] for x in range(wide_x)]
    side_x = [visc[x] + visc[x + 1] for x in range(wide_x - 1)]
    side_y = [visc[x] + north(visc[x]) for x in range(wide_x)]
    side_z = [visc[x] + upper(visc[x]) for x in range(wide_x)]
    corner_xy = [0.25 * (side_y[x] + side_y[x + 1]) for x in range(wide_x - 1)]
    corner_xz = [0.25 * (side_x[x] + upper(side_x[x])) for x in range(wide_x - 1)]
    corner_yz = [0.25 * (side_y[x] + upper(side_y[x])) for x in range(wide_x)]
    rate_x = [(2.0 * VEL_STEP) / side for side in side_x]
    rate_y = [(2.0 * VEL_STEP) / side for side in side_y]
    rate_z = [(2.0 * VEL_STEP) / side for side in side_z]
    moment = [[None] * wide_x for _ in range(3)]
    for sweep in range(ITERS):
        begin, end = sweep, wide_x - sweep
        sig_x, sig_y, sig_z = {}, {}, {}
        tau_xy, tau_xz, tau_yz = {}, {}, {}
        for x in range(begin, end):
            u, v, w = vel[0][x], vel[1][x], vel[2][x]
            if x > begin:
                grad_x = u - vel[0][x - 1]
                grad_y = v - south(v)
                grad_z = w - lower(w)
                div = grad_x + grad_y + grad_z
                press[x] = press[x] - PRESS_STEP * visc[x] * div
                third = div / 3.0
                twice = 2.0 * visc[x]
                sig_x[x] = twice * (grad_x - third) - press[x]
                sig_y[x] = twice * (grad_y - third) - press[x]
                sig_z[x] = twice * (grad_z - third) - press[x]
                tau_yz[x] = jnp.where(
                    in_y, corner_yz[x] * (upper(v) - v + north(w) - w), 0.0
                )
            if x < end - 1:
                inside = in_y & in_x(x)
                tau_xy[x] = jnp.where(
                    inside, corner_xy[x] * (north(u) - u + vel[1][x + 1] - v), 0.0
                )
                tau_xz[x] = jnp.where(
                    in_x(x), corner_xz[x] * (upper(u) - u + vel[2][x + 1] - w), 0.0
                )
        fresh = [[None] * wide_x for _ in range(3)]
        for x in range(begin + 1, end - 1):
            res_x = (
                sig_x[x + 1]
                - sig_x[x]
                + tau_xy[x]
                - south(tau_xy[x])
                + tau_xz[x]
                - lower(tau_xz[x])
            )
            res_y = (
                tau_xy[x]
                - tau_xy[x - 1]
                + north(sig_y[x])
                - sig_y[x]
                + tau_yz[x]
                - lower(tau_yz[x])
            )
            res_z = (
                tau_xz[x]
                - tau_xz[x - 1]
                + tau_yz[x]
                - south(tau_yz[x])
                + upper(sig_z[x])
                - sig_z[x]
                + buoy_ref[x]
            )
            masks = (
                in_y & in_x_face(x),
                in_y_face & in_x(x),
                (in_y & jnp.logical_not(high_lane)) & in_x(x),
            )
            for c, (res, rate, mask) in enumerate(
                zip((res_x, res_y, res_z), (rate_x, rate_y, rate_z), masks)
            ):
                if sweep > 0:
                    res = DAMPING * moment[c][x] + res
                moment[c][x] = res
                fresh[c][x] = jnp.where(mask, vel[c][x] + res * rate[x], 0.0)
        vel = fresh
    for x in range(cells_x):
        for c in range(3):
            new_vel_ref[c, x] = vel[c][x + HALO][HALO : HALO + cells_y]
        new_press_ref[x] = press[x + HALO][HALO : HALO + cells_y]


def stokes(limits, vel, press, buoy, visc, cells_y):
    wide_x, _, num_levels = visc.shape
    cells_x = wide_x - 2 * HALO
    return pl.pallas_call(
        functools.partial(stokes_kernel, cells_y),
        out_shape=(
            jax.ShapeDtypeStruct((3, cells_x, cells_y, num_levels), F32),
            jax.ShapeDtypeStruct((cells_x, cells_y, num_levels), F32),
        ),
        in_specs=[SMEM] + [VMEM] * 4,
        out_specs=(VMEM, VMEM),
        compiler_params=pltpu.CompilerParams(vmem_limit_bytes=48 << 20),
        name="stokes",
    )(limits, vel, press, buoy, visc)


def shifted(x, axis, dim, width):
    devices, length = lax.axis_size(axis), x.shape[dim]
    up = [(i, i + 1) for i in range(devices - 1)]
    down = [(j, i) for i, j in up]
    last = lax.slice_in_dim(x, length - width, length, axis=dim)
    first = lax.slice_in_dim(x, 0, width, axis=dim)
    return lax.ppermute(last, axis, up), lax.ppermute(first, axis, down)


def widened(x):
    before, after = shifted(x, "gx", x.ndim - 3, HALO)
    x = jnp.concatenate([before, x, after], axis=x.ndim - 3)
    before, after = shifted(x, "gy", x.ndim - 2, HALO)
    rows = x.shape[-2] + 2 * HALO
    pad = jnp.zeros(x.shape[:-2] + (-rows % 8, x.shape[-1]), x.dtype)
    return jnp.concatenate([before, x, after, pad], axis=x.ndim - 2)


def shards(
    velocity,
    pressure,
    buoyancy,
    background,
    marker_value,
    marker_height,
    marker_owner,
    marker_column,
    block_count,
):
    cells_x, cells_y, num_levels = pressure.shape
    block_rows, marks = marker_value.shape
    size_x = lax.axis_size("gx")
    size_y = lax.axis_size("gy")
    devices = size_x * size_y
    capacity = max(2, (2 * block_rows + devices - 1) // devices)
    send = deposit(
        block_count,
        marker_owner,
        marker_column,
        marker_value,
        marker_height,
        devices,
        capacity,
        num_levels,
    )
    arrived = lax.all_to_all(
        send.reshape(devices, capacity, 2 * num_levels),
        ("gx", "gy"),
        split_axis=0,
        concat_axis=0,
        tiled=True,
    ).reshape(devices * capacity, 2 * num_levels)
    fields = widened(jnp.concatenate([velocity, pressure[None], buoyancy[None]], axis=0))
    viscosity = gather(arrived, background, marks)
    visc = widened(viscosity)
    limits = jnp.stack(
        [
            lax.axis_index("gx") * cells_x,
            jnp.int32(size_x * cells_x),
            lax.axis_index("gy") * cells_y,
            jnp.int32(size_y * cells_y),
        ]
    ).astype(jnp.int32)
    new_vel, new_press = stokes(limits, fields[:3], fields[3], fields[4], visc, cells_y)
    return (new_vel, new_press, viscosity)


def solution(mesh):
    return jax.shard_map(
        shards,
        mesh=mesh,
        in_specs=(
            P(None, "gx", "gy", None),
            P("gx", "gy", None),
            P("gx", "gy", None),
            P("gx", "gy", None),
            P(("gx", "gy"), None),
            P(("gx", "gy"), None),
            P(("gx", "gy"), None),
            P(("gx", "gy")),
            P(("gx", "gy")),
        ),
        out_specs=(P(None, "gx", "gy", None), P("gx", "gy", None), P("gx", "gy", None)),
        check_vma=False,
    )
```

```python
import functools

import jax
import jax.numpy as jnp
from jax import lax
from jax.experimental import pallas as pl
from jax.experimental.pallas import tpu as pltpu
from jax.sharding import PartitionSpec as P

ITERS = 2
HALO = 2
CHUNKS = 8

PRESS_STEP = 0.5
VEL_STEP = 0.05
DAMPING = 0.8

F32 = jnp.float32
BF16 = jnp.bfloat16
VMEM = pl.BlockSpec(memory_space=pltpu.VMEM)
HBM = pl.BlockSpec(memory_space=pltpu.HBM)
SMEM = pl.BlockSpec(memory_space=pltpu.SMEM)
NT = (((1,), (1,)), ((), ()))
TN = (((0,), (0,)), ((), ()))


def split3(x):
    high = x.astype(BF16)
    rest = x - high.astype(F32)
    mid = rest.astype(BF16)
    low = (rest - mid.astype(F32)).astype(BF16)
    return high, mid, low


def deposit_kernel(
    num_owners,
    capacity,
    count_ref,
    owner_hbm,
    column_hbm,
    value_hbm,
    height_hbm,
    out_ref,
    value_ref,
    height_ref,
    owner_ref,
    column_ref,
    place_ref,
    code_ref,
    part_ref,
    index_sem,
    block_sem,
):
    blocks, marks = value_ref.shape
    num_levels = out_ref.shape[1] // 2
    slots = num_owners * capacity
    chunk = blocks // CHUNKS

    def chunk_copies(k):
        rows = pl.ds(pl.multiple_of(k * chunk, chunk), chunk)
        return (
            pltpu.make_async_copy(height_hbm.at[rows], height_ref.at[rows], block_sem.at[0, k]),
            pltpu.make_async_copy(value_hbm.at[rows], value_ref.at[rows], block_sem.at[1, k]),
        )

    index_copies = (
        pltpu.make_async_copy(owner_hbm, owner_ref, index_sem.at[0]),
        pltpu.make_async_copy(column_hbm, column_ref, index_sem.at[1]),
    )
    for copy in index_copies:
        copy.start()
    for k in range(CHUNKS):
        for copy in chunk_copies(k):
            copy.start()
    for copy in index_copies:
        copy.wait()

    owner = owner_ref[...]
    block_id = lax.broadcasted_iota(jnp.int32, (1, blocks), 1)
    owner = jnp.where(block_id < count_ref[0], owner, num_owners)
    owned = lax.broadcasted_iota(jnp.int32, (num_owners, blocks), 0) == owner
    hits = jnp.where(owned, 1.0, 0.0)
    earlier = jnp.where(
        lax.broadcasted_iota(jnp.int32, (blocks, blocks), 0)
        < lax.broadcasted_iota(jnp.int32, (blocks, blocks), 1),
        1.0,
        0.0,
    ).astype(BF16)
    before = jnp.dot(hits.astype(BF16), earlier, preferred_element_type=F32)
    rank = jnp.sum(hits * before, axis=0, keepdims=True)
    slot = owner * capacity + rank.astype(jnp.int32)
    place = jnp.where(
        lax.broadcasted_iota(jnp.int32, (slots, blocks), 0) == slot, 1.0, 0.0
    ).astype(BF16)
    place_ref[...] = place
    code = jnp.broadcast_to((column_ref[...] + 1).astype(F32), (num_levels, blocks)).astype(BF16)
    code_ref[...] = lax.dot_general(place, code, NT, preferred_element_type=F32)

    row8 = lax.broadcasted_iota(jnp.int32, (8, marks), 0)
    upper_part = (row8 & 1) == 1
    with_value = (row8 & 2) == 0
    leading = row8 < 4
    level = lax.broadcasted_iota(jnp.int32, (num_levels, marks), 0).astype(F32).astype(BF16)

    def one_block(b):
        height = jnp.broadcast_to(height_ref[pl.ds(b, 1), :], (8, marks))
        value = jnp.broadcast_to(value_ref[pl.ds(b, 1), :], (8, marks))
        lower = jnp.minimum(jnp.floor(height), num_levels - 2.0)
        fraction = height - lower
        share = jnp.where(upper_part, fraction, 1.0 - fraction)
        share = share * jnp.where(with_value, value, 1.0)
        high = share.astype(BF16).astype(F32)
        pieces = jnp.where(leading, high, share - high)
        pieces = jnp.concatenate([pieces, pieces], axis=0).astype(BF16)
        lower16 = jnp.concatenate([lower, lower], axis=0).astype(BF16)
        lower_all = jnp.concatenate([lower16] * (num_levels // 16), axis=0)
        hot = jnp.where(lower_all == level, jnp.ones((), BF16), jnp.zeros((), BF16))
        sums = lax.dot_general(pieces, hot, NT, preferred_element_type=F32)
        part_ref[pl.ds(pl.multiple_of(b * 8, 8), 8), :] = sums[:8]

    def one_chunk(k, carry):
        for copy in chunk_copies(k):
            copy.wait()
        for i in range(chunk):
            one_block(k * chunk + i)
        return carry

    lax.fori_loop(0, CHUNKS, one_chunk, 0)

    def part(kind):
        high = part_ref[pl.ds(kind, blocks, stride=8), :]
        return high + part_ref[pl.ds(kind + 4, blocks, stride=8), :]

    value_sum = part(0) + pltpu.roll(part(1), 1, 1)
    weight_sum = part(2) + pltpu.roll(part(3), 1, 1)
    place = place_ref[...]

    def placed(x):
        high, mid, low = (jnp.dot(place, y, preferred_element_type=F32) for y in split3(x))
        return high + (mid + low)

    out_ref[:, :num_levels] = placed(value_sum)
    lane = lax.broadcasted_iota(jnp.int32, (slots, num_levels), 1)
    out_ref[:, num_levels:] = jnp.where(
        lane == num_levels - 1, code_ref[...], placed(weight_sum)
    )


def deposit(count, owner, column, value, height, num_owners, capacity, num_levels):
    blocks, marks = value.shape
    slots = num_owners * capacity
    return pl.pallas_call(
        functools.partial(deposit_kernel, num_owners, capacity),
        out_shape=jax.ShapeDtypeStruct((slots, 2 * num_levels), F32),
        in_specs=[SMEM, HBM, HBM, HBM, HBM],
        out_specs=VMEM,
        scratch_shapes=[
            pltpu.VMEM((blocks, marks), F32),
            pltpu.VMEM((blocks, marks), F32),
            pltpu.VMEM((1, blocks), jnp.int32),
            pltpu.VMEM((1, blocks), jnp.int32),
            pltpu.VMEM((slots, blocks), BF16),
            pltpu.VMEM((slots, num_levels), F32),
            pltpu.VMEM((blocks * 8, num_levels), F32),
            pltpu.SemaphoreType.DMA((2,)),
            pltpu.SemaphoreType.DMA((2, CHUNKS)),
        ],
        compiler_params=pltpu.CompilerParams(vmem_limit_bytes=48 << 20),
        name="deposit",
    )(count, owner.reshape(1, blocks), column.reshape(1, blocks), value, height)


def gather_kernel(marks, odd_ref, arrived_ref, background_ref, out_ref, near_ref, far_ref):
    slots = arrived_ref.shape[0]
    cells_x, cells_y, num_levels = out_ref.shape
    columns = cells_x * cells_y
    values = arrived_ref[:, :num_levels]
    weights = arrived_ref[:, num_levels:]
    lane = lax.broadcasted_iota(jnp.int32, (slots, num_levels), 1)
    last = lane == num_levels - 1
    code = weights[:, num_levels - 1 :]
    others = jnp.sum(jnp.where(last, 0.0, weights), axis=1, keepdims=True)
    weights = jnp.where(last, float(marks) - others, weights)
    place = jnp.where(code == (lane + 1).astype(F32), 1.0, 0.0).astype(BF16)

    def placed(x):
        high, mid, low = (
            lax.dot_general(place, y, TN, preferred_element_type=F32)[:columns] for y in split3(x)
        )
        return high + (mid + low)

    background = background_ref[...].reshape(columns, num_levels)
    visc = jnp.exp((placed(values) + background) / (placed(weights) + 1.0))
    visc = visc.reshape(cells_x, cells_y, num_levels)
    out_ref[...] = visc
    odd = odd_ref[0] == 1
    first, final = visc[:HALO], visc[cells_x - HALO :]
    near_ref[...] = jnp.where(odd, first, final)
    far_ref[...] = jnp.where(odd, final, first)


def gather(odd, arrived, background, marks):
    strip = (HALO,) + background.shape[1:]
    return pl.pallas_call(
        functools.partial(gather_kernel, marks),
        out_shape=(
            jax.ShapeDtypeStruct(background.shape, F32),
            jax.ShapeDtypeStruct(strip, F32),
            jax.ShapeDtypeStruct(strip, F32),
        ),
        in_specs=[SMEM, VMEM, VMEM],
        out_specs=(VMEM, VMEM, VMEM),
        compiler_params=pltpu.CompilerParams(vmem_limit_bytes=48 << 20),
        name="gather",
    )(odd, arrived, background)


def stokes_kernel(
    cells_y,
    limits_ref,
    vel_ref,
    press_ref,
    buoy_ref,
    visc_ref,
    new_vel_ref,
    new_press_ref,
):
    wide_x, rows, num_levels = visc_ref.shape
    cells_x = wide_x - 2 * HALO
    row = lax.broadcasted_iota(jnp.int32, (rows, num_levels), 0)
    lane = lax.broadcasted_iota(jnp.int32, (rows, num_levels), 1)
    first_x, size_x, first_y, size_y = (limits_ref[k] for k in range(4))
    at_y = row + (first_y - HALO)
    in_y = (at_y >= 0) & (at_y < size_y)
    in_y_face = (at_y >= 0) & (at_y < size_y - 1)
    low_lane = lane == 0
    high_lane = lane == num_levels - 1

    def north(f):
        return pltpu.roll(f, rows - 1, 0)

    def south(f):
        return pltpu.roll(f, 1, 0)

    def upper(f):
        return jnp.where(high_lane, 0.0, pltpu.roll(f, num_levels - 1, 1))

    def lower(f):
        return jnp.where(low_lane, 0.0, pltpu.roll(f, 1, 1))

    def in_x(x):
        at_x = first_x - HALO + x
        return (at_x >= 0) & (at_x < size_x)

    def in_x_face(x):
        at_x = first_x - HALO + x
        return (at_x >= 0) & (at_x < size_x - 1)

    inside = [in_y & in_x(x) for x in range(wide_x)]

    def known(ref, x, *lead):
        return jnp.where(inside[x], ref[(*lead, x)], 0.0)

    visc = [known(visc_ref, x) for x in range(wide_x)]
    vel = [[known(vel_ref, x, c) for x in range(wide_x)] for c in range(3)]
    press = [known(press_ref, x) for x in range(wide_x)]
    side_x = [visc[x] + visc[x + 1] for x in range(wide_x - 1)]
    side_y = [visc[x] + north(visc[x]) for x in range(wide_x)]
    side_z = [visc[x] + upper(visc[x]) for x in range(wide_x)]
    corner_xy = [0.25 * (side_y[x] + side_y[x + 1]) for x in range(wide_x - 1)]
    corner_xz = [0.25 * (side_x[x] + upper(side_x[x])) for x in range(wide_x - 1)]
    corner_yz = [0.25 * (side_y[x] + upper(side_y[x])) for x in range(wide_x)]
    rate_x = [(2.0 * VEL_STEP) / side for side in side_x]
    rate_y = [(2.0 * VEL_STEP) / side for side in side_y]
    rate_z = [(2.0 * VEL_STEP) / side for side in side_z]
    moment = [[None] * wide_x for _ in range(3)]
    for sweep in range(ITERS):
        begin, end = sweep, wide_x - sweep
        sig_x, sig_y, sig_z = {}, {}, {}
        tau_xy, tau_xz, tau_yz = {}, {}, {}
        for x in range(begin, end):
            u, v, w = vel[0][x], vel[1][x], vel[2][x]
            if x > begin:
                grad_x = u - vel[0][x - 1]
                grad_y = v - south(v)
                grad_z = w - lower(w)
                div = grad_x + grad_y + grad_z
                press[x] = press[x] - PRESS_STEP * visc[x] * div
                third = div / 3.0
                twice = 2.0 * visc[x]
                sig_x[x] = twice * (grad_x - third) - press[x]
                sig_y[x] = twice * (grad_y - third) - press[x]
                sig_z[x] = twice * (grad_z - third) - press[x]
                tau_yz[x] = jnp.where(
                    in_y, corner_yz[x] * (upper(v) - v + north(w) - w), 0.0
                )
            if x < end - 1:
                tau_xy[x] = jnp.where(
                    inside[x], corner_xy[x] * (north(u) - u + vel[1][x + 1] - v), 0.0
                )
                tau_xz[x] = jnp.where(
                    in_x(x), corner_xz[x] * (upper(u) - u + vel[2][x + 1] - w), 0.0
                )
        fresh = [[None] * wide_x for _ in range(3)]
        for x in range(begin + 1, end - 1):
            res_x = (
                sig_x[x + 1]
                - sig_x[x]
                + tau_xy[x]
                - south(tau_xy[x])
                + tau_xz[x]
                - lower(tau_xz[x])
            )
            res_y = (
                tau_xy[x]
                - tau_xy[x - 1]
                + north(sig_y[x])
                - sig_y[x]
                + tau_yz[x]
                - lower(tau_yz[x])
            )
            res_z = (
                tau_xz[x]
                - tau_xz[x - 1]
                + tau_yz[x]
                - south(tau_yz[x])
                + upper(sig_z[x])
                - sig_z[x]
                + buoy_ref[x]
            )
            masks = (
                in_y & in_x_face(x),
                in_y_face & in_x(x),
                (in_y & jnp.logical_not(high_lane)) & in_x(x),
            )
            for c, (res, rate, mask) in enumerate(
                zip((res_x, res_y, res_z), (rate_x, rate_y, rate_z), masks)
            ):
                if sweep > 0:
                    res = DAMPING * moment[c][x] + res
                moment[c][x] = res
                fresh[c][x] = jnp.where(mask, vel[c][x] + res * rate[x], 0.0)
        vel = fresh
    for x in range(cells_x):
        for c in range(3):
            new_vel_ref[c, x] = vel[c][x + HALO][HALO : HALO + cells_y]
        new_press_ref[x] = press[x + HALO][HALO : HALO + cells_y]


def stokes(limits, vel, press, buoy, visc, cells_y):
    wide_x, _, num_levels = visc.shape
    cells_x = wide_x - 2 * HALO
    return pl.pallas_call(
        functools.partial(stokes_kernel, cells_y),
        out_shape=(
            jax.ShapeDtypeStruct((3, cells_x, cells_y, num_levels), F32),
            jax.ShapeDtypeStruct((cells_x, cells_y, num_levels), F32),
        ),
        in_specs=[SMEM] + [VMEM] * 4,
        out_specs=(VMEM, VMEM),
        compiler_params=pltpu.CompilerParams(vmem_limit_bytes=48 << 20),
        name="stokes",
    )(limits, vel, press, buoy, visc)


def partners(size_x, size_y):
    def flat(x, y):
        return (x % size_x) * size_y + y

    cells = [(x, y) for x in range(size_x) for y in range(size_y)]
    x_near = [(flat(x, y), flat(x ^ 1, y)) for x, y in cells]
    x_far = [(flat(x, y), flat(x + 1 if x % 2 else x - 1, y)) for x, y in cells]
    y_near = [(flat(x, y), flat(x, y ^ 1)) for x, y in cells]
    y_far = [
        (flat(x, y), flat(x ^ 1, y) if y in (0, size_y - 1) else flat(x, y + 1 if y % 2 else y - 1))
        for x, y in cells
    ]
    return x_near, x_far, y_near, y_far


def swapped(near, far, near_pairs, far_pairs, odd, dim, x):
    near = lax.ppermute(near, ("gx", "gy"), near_pairs)
    far = lax.ppermute(far, ("gx", "gy"), far_pairs)
    before, after = jnp.where(odd, near, far), jnp.where(odd, far, near)
    return jnp.concatenate([before, x, after], axis=dim)


def strips(x, odd, dim):
    length = x.shape[dim]
    first = lax.slice_in_dim(x, 0, HALO, axis=dim)
    final = lax.slice_in_dim(x, length - HALO, length, axis=dim)
    return jnp.where(odd, first, final), jnp.where(odd, final, first)


def widened(x, near, far, pairs, odd_x, odd_y):
    dim = x.ndim - 3
    x = swapped(near, far, pairs[0], pairs[1], odd_x, dim, x)
    x = swapped(*strips(x, odd_y, dim + 1), pairs[2], pairs[3], odd_y, dim + 1, x)
    pad = jnp.zeros(x.shape[:-2] + (-x.shape[-2] % 8, x.shape[-1]), x.dtype)
    return jnp.concatenate([x, pad], axis=dim + 1)


def shards(
    velocity,
    pressure,
    buoyancy,
    background,
    marker_value,
    marker_height,
    marker_owner,
    marker_column,
    block_count,
):
    cells_x, cells_y, num_levels = pressure.shape
    block_rows, marks = marker_value.shape
    size_x = lax.axis_size("gx")
    size_y = lax.axis_size("gy")
    devices = size_x * size_y
    capacity = max(2, (2 * block_rows + devices - 1) // devices)
    send = deposit(
        block_count,
        marker_owner,
        marker_column,
        marker_value,
        marker_height,
        devices,
        capacity,
        num_levels,
    )
    arrived = lax.all_to_all(
        send.reshape(devices, capacity, 2 * num_levels),
        ("gx", "gy"),
        split_axis=0,
        concat_axis=0,
        tiled=True,
    ).reshape(devices * capacity, 2 * num_levels)
    pairs = partners(size_x, size_y)
    odd_x = lax.axis_index("gx") % 2
    odd_y = lax.axis_index("gy") % 2
    fields = jnp.concatenate([velocity, pressure[None], buoyancy[None]], axis=0)
    fields = widened(fields, *strips(fields, odd_x == 1, 1), pairs, odd_x == 1, odd_y == 1)
    viscosity, near, far = gather(odd_x.astype(jnp.int32)[None], arrived, background, marks)
    visc = widened(viscosity, near, far, pairs, odd_x == 1, odd_y == 1)
    limits = jnp.stack(
        [
            lax.axis_index("gx") * cells_x,
            jnp.int32(size_x * cells_x),
            lax.axis_index("gy") * cells_y,
            jnp.int32(size_y * cells_y),
        ]
    ).astype(jnp.int32)
    new_vel, new_press = stokes(limits, fields[:3], fields[3], fields[4], visc, cells_y)
    return (new_vel, new_press, viscosity)


def solution(mesh):
    return jax.shard_map(
        shards,
        mesh=mesh,
        in_specs=(
            P(None, "gx", "gy", None),
            P("gx", "gy", None),
            P("gx", "gy", None),
            P("gx", "gy", None),
            P(("gx", "gy"), None),
            P(("gx", "gy"), None),
            P(("gx", "gy"), None),
            P(("gx", "gy")),
            P(("gx", "gy")),
        ),
        out_specs=(P(None, "gx", "gy", None), P("gx", "gy", None), P("gx", "gy", None)),
        check_vma=False,
    )
```

```python
import functools

import jax
import jax.numpy as jnp
from jax import lax
from jax.experimental import pallas as pl
from jax.experimental.pallas import tpu as pltpu
from jax.sharding import PartitionSpec as P

ITERS = 2
HALO = 2
CHUNKS = 4
WAYS = 4
OUT_PARTS = 2

PRESS_STEP = 0.5
VEL_STEP = 0.05
DAMPING = 0.8

F32 = jnp.float32
BF16 = jnp.bfloat16
VMEM = pl.BlockSpec(memory_space=pltpu.VMEM)
HBM = pl.BlockSpec(memory_space=pltpu.HBM)
SMEM = pl.BlockSpec(memory_space=pltpu.SMEM)
NT = (((1,), (1,)), ((), ()))


def split3(x):
    high = x.astype(BF16)
    rest = x - high.astype(F32)
    mid = rest.astype(BF16)
    low = (rest - mid.astype(F32)).astype(BF16)
    return high, mid, low


def deposit_kernel(
    num_owners,
    capacity,
    count_ref,
    owner_hbm,
    column_hbm,
    value_hbm,
    height_hbm,
    out_hbm,
    value_ref,
    height_ref,
    owner_ref,
    column_ref,
    place_ref,
    code_ref,
    lower_ref,
    fraction_ref,
    part_ref,
    out_ref,
    index_sem,
    block_sem,
    out_sem,
):
    blocks, marks = value_ref.shape
    num_levels = out_ref.shape[1] // 2
    slots = num_owners * capacity
    chunk = blocks // CHUNKS

    def chunk_copies(k):
        rows = pl.ds(pl.multiple_of(k * chunk, chunk), chunk)
        return (
            pltpu.make_async_copy(height_hbm.at[rows], height_ref.at[rows], block_sem.at[0, k]),
            pltpu.make_async_copy(value_hbm.at[rows], value_ref.at[rows], block_sem.at[1, k]),
        )

    index_copies = (
        pltpu.make_async_copy(owner_hbm, owner_ref, index_sem.at[0]),
        pltpu.make_async_copy(column_hbm, column_ref, index_sem.at[1]),
    )
    for copy in index_copies:
        copy.start()
    for k in range(CHUNKS):
        for copy in chunk_copies(k):
            copy.start()
    for copy in index_copies:
        copy.wait()

    owner = owner_ref[...]
    block_id = lax.broadcasted_iota(jnp.int32, (1, blocks), 1)
    owner = jnp.where(block_id < count_ref[0], owner, num_owners)
    owned = lax.broadcasted_iota(jnp.int32, (num_owners, blocks), 0) == owner
    hits = jnp.where(owned, 1.0, 0.0)
    earlier = jnp.where(
        lax.broadcasted_iota(jnp.int32, (blocks, blocks), 0)
        < lax.broadcasted_iota(jnp.int32, (blocks, blocks), 1),
        1.0,
        0.0,
    ).astype(BF16)
    before = jnp.dot(hits.astype(BF16), earlier, preferred_element_type=F32)
    rank = jnp.sum(hits * before, axis=0, keepdims=True)
    slot = owner * capacity + rank.astype(jnp.int32)
    place = jnp.where(
        lax.broadcasted_iota(jnp.int32, (slots, blocks), 0) == slot, 1.0, 0.0
    ).astype(BF16)
    place_ref[...] = place
    code = jnp.broadcast_to((column_ref[...] + 1).astype(F32), (num_levels, blocks)).astype(BF16)
    code_ref[...] = lax.dot_general(place, code, NT, preferred_element_type=F32)

    span = num_levels // WAYS
    row8 = lax.broadcasted_iota(jnp.int32, (8, marks), 0)
    upper_part = (row8 & 1) == 1
    with_value = (row8 & 2) == 0
    leading = row8 < 4
    offset_id = lax.broadcasted_iota(jnp.int32, (span, marks), 0).astype(F32).astype(BF16)
    lane_window = lax.broadcasted_iota(jnp.int32, (8, num_levels), 1) // span

    def operands(b):
        lower = jnp.broadcast_to(lower_ref[pl.ds(b, 1), :], (8, marks))
        fraction = jnp.broadcast_to(fraction_ref[pl.ds(b, 1), :], (8, marks))
        value = jnp.broadcast_to(value_ref[pl.ds(b, 1), :], (8, marks))
        share = jnp.where(upper_part, fraction, 1.0 - fraction)
        share = share * jnp.where(with_value, value, 1.0)
        high = share.astype(BF16).astype(F32)
        pieces = jnp.where(leading, high, share - high)
        window = jnp.floor(lower * (1.0 / span))
        offset = lower - window * span
        offset = jnp.concatenate([offset, offset], axis=0).astype(BF16)
        offset = jnp.concatenate([offset] * (span // 16), axis=0)
        hot = jnp.where(offset == offset_id, jnp.ones((), BF16), jnp.zeros((), BF16))
        return [jnp.where(window == a, pieces, 0.0) for a in range(WAYS)], hot

    def one_chunk(k, carry):
        for copy in chunk_copies(k):
            copy.wait()
        rows = pl.ds(pl.multiple_of(k * chunk, chunk), chunk)
        height = height_ref[rows, :]
        lower = jnp.minimum(jnp.floor(height), num_levels - 2.0)
        lower_ref[rows, :] = lower
        fraction_ref[rows, :] = height - lower
        for first in range(0, chunk, WAYS):
            b = k * chunk + first
            pieces, hots = zip(*(operands(b + i) for i in range(WAYS)))
            sums = lax.dot_general(
                jnp.concatenate(sum(pieces, []), axis=0).astype(BF16),
                jnp.concatenate(hots, axis=0),
                NT,
                preferred_element_type=F32,
            )
            for i in range(WAYS):
                total = jnp.zeros((8, num_levels), F32)
                for a in range(WAYS):
                    found = sums[(i * WAYS + a) * 8 : (i * WAYS + a + 1) * 8]
                    turn = ((a - i) * span) % num_levels
                    found = pltpu.roll(found, turn, 1) if turn else found
                    total = jnp.where(lane_window == a, found, total)
                part_ref[pl.ds(pl.multiple_of((b + i) * 8, 8), 8), :] = total
        return carry

    lax.fori_loop(0, CHUNKS, one_chunk, 0)

    def part(kind):
        high = part_ref[pl.ds(kind, blocks, stride=8), :]
        return high + part_ref[pl.ds(kind + 4, blocks, stride=8), :]

    value_sum = part(0) + pltpu.roll(part(1), 1, 1)
    weight_sum = part(2) + pltpu.roll(part(3), 1, 1)
    pieces = split3(jnp.concatenate([value_sum, weight_sum], axis=1))
    size = slots // OUT_PARTS
    copies = []
    for p in range(OUT_PARTS):
        rows = slice(p * size, (p + 1) * size)
        high, mid, low = (
            jnp.dot(place_ref[rows], y, preferred_element_type=F32) for y in pieces
        )
        sums = high + (mid + low)
        lane = lax.broadcasted_iota(jnp.int32, (size, num_levels), 1)
        out_ref[rows, :num_levels] = sums[:, :num_levels]
        out_ref[rows, num_levels:] = jnp.where(
            lane == num_levels - 1, code_ref[rows], sums[:, num_levels:]
        )
        copy = pltpu.make_async_copy(out_ref.at[rows], out_hbm.at[rows], out_sem.at[p])
        copy.start()
        copies.append(copy)
    for copy in copies:
        copy.wait()


def deposit(count, owner, column, value, height, num_owners, capacity, num_levels):
    blocks, marks = value.shape
    slots = num_owners * capacity
    return pl.pallas_call(
        functools.partial(deposit_kernel, num_owners, capacity),
        out_shape=jax.ShapeDtypeStruct((slots, 2 * num_levels), F32),
        in_specs=[SMEM, HBM, HBM, HBM, HBM],
        out_specs=HBM,
        scratch_shapes=[
            pltpu.VMEM((blocks, marks), F32),
            pltpu.VMEM((blocks, marks), F32),
            pltpu.VMEM((1, blocks), jnp.int32),
            pltpu.VMEM((1, blocks), jnp.int32),
            pltpu.VMEM((slots, blocks), BF16),
            pltpu.VMEM((slots, num_levels), F32),
            pltpu.VMEM((blocks, marks), F32),
            pltpu.VMEM((blocks, marks), F32),
            pltpu.VMEM((blocks * 8, num_levels), F32),
            pltpu.VMEM((slots, 2 * num_levels), F32),
            pltpu.SemaphoreType.DMA((2,)),
            pltpu.SemaphoreType.DMA((2, CHUNKS)),
            pltpu.SemaphoreType.DMA((OUT_PARTS,)),
        ],
        compiler_params=pltpu.CompilerParams(vmem_limit_bytes=60 << 20),
        name="deposit",
    )(count, owner.reshape(1, blocks), column.reshape(1, blocks), value, height)


def gather_kernel(marks, odd_ref, arrived_ref, background_ref, out_ref, near_ref, far_ref):
    slots = arrived_ref.shape[0]
    cells_x, cells_y, num_levels = out_ref.shape
    columns = cells_x * cells_y
    values = arrived_ref[:, :num_levels]
    weights = arrived_ref[:, num_levels:]
    last = lax.broadcasted_iota(jnp.int32, (slots, num_levels), 1) == num_levels - 1
    pick = jnp.where(
        lax.broadcasted_iota(jnp.int32, (8, num_levels), 1) == num_levels - 1, 1.0, 0.0
    ).astype(BF16)
    column_id = (lax.broadcasted_iota(jnp.int32, (columns, slots), 0) + 1).astype(F32)
    codes = lax.dot_general(pick, weights.astype(BF16), NT, preferred_element_type=F32)
    place = jnp.where(codes[:1] == column_id, 1.0, 0.0).astype(BF16)
    others = jnp.sum(jnp.where(last, 0.0, weights), axis=1, keepdims=True)
    weights = jnp.where(last, float(marks) - others, weights)
    high, mid, low = (
        jnp.dot(place, y, preferred_element_type=F32)
        for y in split3(jnp.concatenate([values, weights], axis=1))
    )
    sums = high + (mid + low)
    background = background_ref[...].reshape(columns, num_levels)
    visc = jnp.exp((sums[:, :num_levels] + background) / (sums[:, num_levels:] + 1.0))
    visc = visc.reshape(cells_x, cells_y, num_levels)
    out_ref[...] = visc
    odd = odd_ref[0] == 1
    first, final = visc[:HALO], visc[cells_x - HALO :]
    near_ref[...] = jnp.where(odd, first, final)
    far_ref[...] = jnp.where(odd, final, first)


def gather(odd, arrived, background, marks):
    strip = (HALO,) + background.shape[1:]
    return pl.pallas_call(
        functools.partial(gather_kernel, marks),
        out_shape=(
            jax.ShapeDtypeStruct(background.shape, F32),
            jax.ShapeDtypeStruct(strip, F32),
            jax.ShapeDtypeStruct(strip, F32),
        ),
        in_specs=[SMEM, VMEM, VMEM],
        out_specs=(VMEM, VMEM, VMEM),
        compiler_params=pltpu.CompilerParams(vmem_limit_bytes=48 << 20),
        name="gather",
    )(odd, arrived, background)


def stokes_kernel(
    cells_y,
    limits_ref,
    vel_ref,
    press_ref,
    buoy_ref,
    visc_ref,
    new_vel_ref,
    new_press_ref,
):
    wide_x, rows, num_levels = visc_ref.shape
    cells_x = wide_x - 2 * HALO
    row = lax.broadcasted_iota(jnp.int32, (rows, num_levels), 0)
    lane = lax.broadcasted_iota(jnp.int32, (rows, num_levels), 1)
    first_x, size_x, first_y, size_y = (limits_ref[k] for k in range(4))
    at_y = row + (first_y - HALO)
    in_y = (at_y >= 0) & (at_y < size_y)
    in_y_face = (at_y >= 0) & (at_y < size_y - 1)
    low_lane = lane == 0
    high_lane = lane == num_levels - 1

    def north(f):
        return pltpu.roll(f, rows - 1, 0)

    def south(f):
        return pltpu.roll(f, 1, 0)

    def upper(f):
        return jnp.where(high_lane, 0.0, pltpu.roll(f, num_levels - 1, 1))

    def lower(f):
        return jnp.where(low_lane, 0.0, pltpu.roll(f, 1, 1))

    def in_x(x):
        at_x = first_x - HALO + x
        return (at_x >= 0) & (at_x < size_x)

    def in_x_face(x):
        at_x = first_x - HALO + x
        return (at_x >= 0) & (at_x < size_x - 1)

    inside = [in_y & in_x(x) for x in range(wide_x)]

    def known(ref, x, *lead):
        return jnp.where(inside[x], ref[(*lead, x)], 0.0)

    visc = [known(visc_ref, x) for x in range(wide_x)]
    vel = [[known(vel_ref, x, c) for x in range(wide_x)] for c in range(3)]
    press = [known(press_ref, x) for x in range(wide_x)]
    side_x = [visc[x] + visc[x + 1] for x in range(wide_x - 1)]
    side_y = [visc[x] + north(visc[x]) for x in range(wide_x)]
    side_z = [visc[x] + upper(visc[x]) for x in range(wide_x)]
    corner_xy = [0.25 * (side_y[x] + side_y[x + 1]) for x in range(wide_x - 1)]
    corner_xz = [0.25 * (side_x[x] + upper(side_x[x])) for x in range(wide_x - 1)]
    corner_yz = [0.25 * (side_y[x] + upper(side_y[x])) for x in range(wide_x)]
    rate_x = [(2.0 * VEL_STEP) / side for side in side_x]
    rate_y = [(2.0 * VEL_STEP) / side for side in side_y]
    rate_z = [(2.0 * VEL_STEP) / side for side in side_z]
    moment = [[None] * wide_x for _ in range(3)]
    for sweep in range(ITERS):
        begin, end = sweep, wide_x - sweep
        sig_x, sig_y, sig_z = {}, {}, {}
        tau_xy, tau_xz, tau_yz = {}, {}, {}
        for x in range(begin, end):
            u, v, w = vel[0][x], vel[1][x], vel[2][x]
            if x > begin:
                grad_x = u - vel[0][x - 1]
                grad_y = v - south(v)
                grad_z = w - lower(w)
                div = grad_x + grad_y + grad_z
                press[x] = press[x] - PRESS_STEP * visc[x] * div
                third = div / 3.0
                twice = 2.0 * visc[x]
                sig_x[x] = twice * (grad_x - third) - press[x]
                sig_y[x] = twice * (grad_y - third) - press[x]
                sig_z[x] = twice * (grad_z - third) - press[x]
                tau_yz[x] = jnp.where(
                    in_y, corner_yz[x] * (upper(v) - v + north(w) - w), 0.0
                )
            if x < end - 1:
                tau_xy[x] = jnp.where(
                    inside[x], corner_xy[x] * (north(u) - u + vel[1][x + 1] - v), 0.0
                )
                tau_xz[x] = jnp.where(
                    in_x(x), corner_xz[x] * (upper(u) - u + vel[2][x + 1] - w), 0.0
                )
        fresh = [[None] * wide_x for _ in range(3)]
        for x in range(begin + 1, end - 1):
            res_x = (
                sig_x[x + 1]
                - sig_x[x]
                + tau_xy[x]
                - south(tau_xy[x])
                + tau_xz[x]
                - lower(tau_xz[x])
            )
            res_y = (
                tau_xy[x]
                - tau_xy[x - 1]
                + north(sig_y[x])
                - sig_y[x]
                + tau_yz[x]
                - lower(tau_yz[x])
            )
            res_z = (
                tau_xz[x]
                - tau_xz[x - 1]
                + tau_yz[x]
                - south(tau_yz[x])
                + upper(sig_z[x])
                - sig_z[x]
                + buoy_ref[x]
            )
            masks = (
                in_y & in_x_face(x),
                in_y_face & in_x(x),
                (in_y & jnp.logical_not(high_lane)) & in_x(x),
            )
            for c, (res, rate, mask) in enumerate(
                zip((res_x, res_y, res_z), (rate_x, rate_y, rate_z), masks)
            ):
                if sweep > 0:
                    res = DAMPING * moment[c][x] + res
                moment[c][x] = res
                fresh[c][x] = jnp.where(mask, vel[c][x] + res * rate[x], 0.0)
        vel = fresh
    for x in range(cells_x):
        for c in range(3):
            new_vel_ref[c, x] = vel[c][x + HALO][HALO : HALO + cells_y]
        new_press_ref[x] = press[x + HALO][HALO : HALO + cells_y]


def stokes(limits, vel, press, buoy, visc, cells_y):
    wide_x, _, num_levels = visc.shape
    cells_x = wide_x - 2 * HALO
    return pl.pallas_call(
        functools.partial(stokes_kernel, cells_y),
        out_shape=(
            jax.ShapeDtypeStruct((3, cells_x, cells_y, num_levels), F32),
            jax.ShapeDtypeStruct((cells_x, cells_y, num_levels), F32),
        ),
        in_specs=[SMEM] + [VMEM] * 4,
        out_specs=(VMEM, VMEM),
        compiler_params=pltpu.CompilerParams(vmem_limit_bytes=48 << 20),
        name="stokes",
    )(limits, vel, press, buoy, visc)


def partners(size_x, size_y):
    def flat(x, y):
        return (x % size_x) * size_y + y

    cells = [(x, y) for x in range(size_x) for y in range(size_y)]
    x_near = [(flat(x, y), flat(x ^ 1, y)) for x, y in cells]
    x_far = [(flat(x, y), flat(x + 1 if x % 2 else x - 1, y)) for x, y in cells]
    y_near = [(flat(x, y), flat(x, y ^ 1)) for x, y in cells]
    y_far = [
        (flat(x, y), flat(x ^ 1, y) if y in (0, size_y - 1) else flat(x, y + 1 if y % 2 else y - 1))
        for x, y in cells
    ]
    return x_near, x_far, y_near, y_far


def swapped(near, far, near_pairs, far_pairs, odd, dim, x):
    near = lax.ppermute(near, ("gx", "gy"), near_pairs)
    far = lax.ppermute(far, ("gx", "gy"), far_pairs)
    before, after = jnp.where(odd, near, far), jnp.where(odd, far, near)
    return jnp.concatenate([before, x, after], axis=dim)


def strips(x, odd, dim):
    length = x.shape[dim]
    first = lax.slice_in_dim(x, 0, HALO, axis=dim)
    final = lax.slice_in_dim(x, length - HALO, length, axis=dim)
    return jnp.where(odd, first, final), jnp.where(odd, final, first)


def widened(x, near, far, pairs, odd_x, odd_y):
    dim = x.ndim - 3
    x = swapped(near, far, pairs[0], pairs[1], odd_x, dim, x)
    x = swapped(*strips(x, odd_y, dim + 1), pairs[2], pairs[3], odd_y, dim + 1, x)
    pad = jnp.zeros(x.shape[:-2] + (-x.shape[-2] % 8, x.shape[-1]), x.dtype)
    return jnp.concatenate([x, pad], axis=dim + 1)


def shards(
    velocity,
    pressure,
    buoyancy,
    background,
    marker_value,
    marker_height,
    marker_owner,
    marker_column,
    block_count,
):
    cells_x, cells_y, num_levels = pressure.shape
    block_rows, marks = marker_value.shape
    size_x = lax.axis_size("gx")
    size_y = lax.axis_size("gy")
    devices = size_x * size_y
    capacity = max(2, (2 * block_rows + devices - 1) // devices)
    send = deposit(
        block_count,
        marker_owner,
        marker_column,
        marker_value,
        marker_height,
        devices,
        capacity,
        num_levels,
    )
    arrived = lax.all_to_all(
        send.reshape(devices, capacity, 2 * num_levels),
        ("gx", "gy"),
        split_axis=0,
        concat_axis=0,
        tiled=True,
    ).reshape(devices * capacity, 2 * num_levels)
    pairs = partners(size_x, size_y)
    odd_x = lax.axis_index("gx") % 2
    odd_y = lax.axis_index("gy") % 2
    fields = jnp.concatenate([velocity, pressure[None], buoyancy[None]], axis=0)
    fields = widened(fields, *strips(fields, odd_x == 1, 1), pairs, odd_x == 1, odd_y == 1)
    viscosity, near, far = gather(odd_x.astype(jnp.int32)[None], arrived, background, marks)
    visc = widened(viscosity, near, far, pairs, odd_x == 1, odd_y == 1)
    limits = jnp.stack(
        [
            lax.axis_index("gx") * cells_x,
            jnp.int32(size_x * cells_x),
            lax.axis_index("gy") * cells_y,
            jnp.int32(size_y * cells_y),
        ]
    ).astype(jnp.int32)
    new_vel, new_press = stokes(limits, fields[:3], fields[3], fields[4], visc, cells_y)
    return (new_vel, new_press, viscosity)


def solution(mesh):
    return jax.shard_map(
        shards,
        mesh=mesh,
        in_specs=(
            P(None, "gx", "gy", None),
            P("gx", "gy", None),
            P("gx", "gy", None),
            P("gx", "gy", None),
            P(("gx", "gy"), None),
            P(("gx", "gy"), None),
            P(("gx", "gy"), None),
            P(("gx", "gy")),
            P(("gx", "gy")),
        ),
        out_specs=(P(None, "gx", "gy", None), P("gx", "gy", None), P("gx", "gy", None)),
        check_vma=False,
    )
```

```python
import functools

import jax
import jax.numpy as jnp
from jax import lax
from jax.experimental import pallas as pl
from jax.experimental.pallas import tpu as pltpu
from jax.sharding import PartitionSpec as P

ITERS = 2
HALO = 2
CHUNKS = 1
WAYS = 4
OUT_PARTS = 2

PRESS_STEP = 0.5
VEL_STEP = 0.05
DAMPING = 0.8

F32 = jnp.float32
BF16 = jnp.bfloat16
VMEM = pl.BlockSpec(memory_space=pltpu.VMEM)
HBM = pl.BlockSpec(memory_space=pltpu.HBM)
SMEM = pl.BlockSpec(memory_space=pltpu.SMEM)
NT = (((1,), (1,)), ((), ()))


def split3(x):
    high = x.astype(BF16)
    rest = x - high.astype(F32)
    mid = rest.astype(BF16)
    low = (rest - mid.astype(F32)).astype(BF16)
    return high, mid, low


def deposit_kernel(
    num_owners,
    capacity,
    count_ref,
    owner_hbm,
    column_hbm,
    value_hbm,
    height_hbm,
    out_hbm,
    value_ref,
    height_ref,
    owner_ref,
    column_ref,
    place_ref,
    code_ref,
    lower_ref,
    fraction_ref,
    part_ref,
    out_ref,
    index_sem,
    block_sem,
    out_sem,
):
    blocks, marks = value_ref.shape
    num_levels = out_ref.shape[1] // 2
    slots = num_owners * capacity
    chunk = blocks // CHUNKS

    def chunk_copies(k):
        rows = pl.ds(pl.multiple_of(k * chunk, chunk), chunk)
        return (
            pltpu.make_async_copy(height_hbm.at[rows], height_ref.at[rows], block_sem.at[0, k]),
            pltpu.make_async_copy(value_hbm.at[rows], value_ref.at[rows], block_sem.at[1, k]),
        )

    index_copies = (
        pltpu.make_async_copy(owner_hbm, owner_ref, index_sem.at[0]),
        pltpu.make_async_copy(column_hbm, column_ref, index_sem.at[1]),
    )
    for copy in index_copies:
        copy.start()
    for k in range(CHUNKS):
        for copy in chunk_copies(k):
            copy.start()
    for copy in index_copies:
        copy.wait()

    owner = owner_ref[...]
    block_id = lax.broadcasted_iota(jnp.int32, (1, blocks), 1)
    owner = jnp.where(block_id < count_ref[0], owner, num_owners)
    owned = lax.broadcasted_iota(jnp.int32, (num_owners, blocks), 0) == owner
    hits = jnp.where(owned, 1.0, 0.0)
    earlier = jnp.where(
        lax.broadcasted_iota(jnp.int32, (blocks, blocks), 0)
        < lax.broadcasted_iota(jnp.int32, (blocks, blocks), 1),
        1.0,
        0.0,
    ).astype(BF16)
    before = jnp.dot(hits.astype(BF16), earlier, preferred_element_type=F32)
    rank = jnp.sum(hits * before, axis=0, keepdims=True)
    slot = owner * capacity + rank.astype(jnp.int32)
    place = jnp.where(
        lax.broadcasted_iota(jnp.int32, (slots, blocks), 0) == slot, 1.0, 0.0
    ).astype(BF16)
    place_ref[...] = place
    code = jnp.broadcast_to((column_ref[...] + 1).astype(F32), (num_levels, blocks)).astype(BF16)
    code_ref[...] = lax.dot_general(place, code, NT, preferred_element_type=F32)

    span = num_levels // WAYS
    row8 = lax.broadcasted_iota(jnp.int32, (8, marks), 0)
    upper_part = (row8 & 1) == 1
    with_value = (row8 & 2) == 0
    leading = row8 < 4
    offset_id = lax.broadcasted_iota(jnp.int32, (span, marks), 0).astype(F32).astype(BF16)
    lane_window = lax.broadcasted_iota(jnp.int32, (8, num_levels), 1) // span

    def operands(b):
        lower = jnp.broadcast_to(lower_ref[pl.ds(b, 1), :], (8, marks))
        fraction = jnp.broadcast_to(fraction_ref[pl.ds(b, 1), :], (8, marks))
        value = jnp.broadcast_to(value_ref[pl.ds(b, 1), :], (8, marks))
        share = jnp.where(upper_part, fraction, 1.0 - fraction)
        share = share * jnp.where(with_value, value, 1.0)
        high = share.astype(BF16).astype(F32)
        pieces = jnp.where(leading, high, share - high)
        window = jnp.floor(lower * (1.0 / span))
        offset = lower - window * span
        offset = jnp.concatenate([offset, offset], axis=0).astype(BF16)
        offset = jnp.concatenate([offset] * (span // 16), axis=0)
        hot = jnp.where(offset == offset_id, jnp.ones((), BF16), jnp.zeros((), BF16))
        return [jnp.where(window == a, pieces, 0.0) for a in range(WAYS)], hot

    def one_chunk(k, carry):
        for copy in chunk_copies(k):
            copy.wait()
        rows = pl.ds(pl.multiple_of(k * chunk, chunk), chunk)
        height = height_ref[rows, :]
        lower = jnp.minimum(jnp.floor(height), num_levels - 2.0)
        lower_ref[rows, :] = lower
        fraction_ref[rows, :] = height - lower
        for first in range(0, chunk, WAYS):
            b = k * chunk + first
            pieces, hots = zip(*(operands(b + i) for i in range(WAYS)))
            sums = lax.dot_general(
                jnp.concatenate(sum(pieces, []), axis=0).astype(BF16),
                jnp.concatenate(hots, axis=0),
                NT,
                preferred_element_type=F32,
            )
            for i in range(WAYS):
                total = jnp.zeros((8, num_levels), F32)
                for a in range(WAYS):
                    found = sums[(i * WAYS + a) * 8 : (i * WAYS + a + 1) * 8]
                    turn = ((a - i) * span) % num_levels
                    found = pltpu.roll(found, turn, 1) if turn else found
                    total = jnp.where(lane_window == a, found, total)
                part_ref[pl.ds(pl.multiple_of((b + i) * 8, 8), 8), :] = total
        return carry

    lax.fori_loop(0, CHUNKS, one_chunk, 0)

    def part(kind):
        high = part_ref[pl.ds(kind, blocks, stride=8), :]
        return high + part_ref[pl.ds(kind + 4, blocks, stride=8), :]

    value_sum = part(0) + pltpu.roll(part(1), 1, 1)
    weight_sum = part(2) + pltpu.roll(part(3), 1, 1)
    pieces = split3(jnp.concatenate([value_sum, weight_sum], axis=1))
    size = slots // OUT_PARTS
    copies = []
    for p in range(OUT_PARTS):
        rows = slice(p * size, (p + 1) * size)
        high, mid, low = (
            jnp.dot(place_ref[rows], y, preferred_element_type=F32) for y in pieces
        )
        sums = high + (mid + low)
        lane = lax.broadcasted_iota(jnp.int32, (size, num_levels), 1)
        out_ref[rows, :num_levels] = sums[:, :num_levels]
        out_ref[rows, num_levels:] = jnp.where(
            lane == num_levels - 1, code_ref[rows], sums[:, num_levels:]
        )
        copy = pltpu.make_async_copy(out_ref.at[rows], out_hbm.at[rows], out_sem.at[p])
        copy.start()
        copies.append(copy)
    for copy in copies:
        copy.wait()


def deposit(count, owner, column, value, height, num_owners, capacity, num_levels):
    blocks, marks = value.shape
    slots = num_owners * capacity
    return pl.pallas_call(
        functools.partial(deposit_kernel, num_owners, capacity),
        out_shape=jax.ShapeDtypeStruct((slots, 2 * num_levels), F32),
        in_specs=[SMEM, HBM, HBM, HBM, HBM],
        out_specs=HBM,
        scratch_shapes=[
            pltpu.VMEM((blocks, marks), F32),
            pltpu.VMEM((blocks, marks), F32),
            pltpu.VMEM((1, blocks), jnp.int32),
            pltpu.VMEM((1, blocks), jnp.int32),
            pltpu.VMEM((slots, blocks), BF16),
            pltpu.VMEM((slots, num_levels), F32),
            pltpu.VMEM((blocks, marks), F32),
            pltpu.VMEM((blocks, marks), F32),
            pltpu.VMEM((blocks * 8, num_levels), F32),
            pltpu.VMEM((slots, 2 * num_levels), F32),
            pltpu.SemaphoreType.DMA((2,)),
            pltpu.SemaphoreType.DMA((2, CHUNKS)),
            pltpu.SemaphoreType.DMA((OUT_PARTS,)),
        ],
        compiler_params=pltpu.CompilerParams(vmem_limit_bytes=60 << 20),
        name="deposit",
    )(count, owner.reshape(1, blocks), column.reshape(1, blocks), value, height)


def gather_kernel(marks, here_ref, arrived_ref, background_ref, out_ref, near_ref, far_ref):
    slots = arrived_ref.shape[0]
    cells_x, cells_y, num_levels = out_ref.shape
    columns = cells_x * cells_y
    values = arrived_ref[:, :num_levels]
    weights = arrived_ref[:, num_levels:]
    last = lax.broadcasted_iota(jnp.int32, (slots, num_levels), 1) == num_levels - 1
    pick = jnp.where(
        lax.broadcasted_iota(jnp.int32, (8, num_levels), 1) == num_levels - 1, 1.0, 0.0
    ).astype(BF16)
    column_id = (lax.broadcasted_iota(jnp.int32, (columns, slots), 0) + 1).astype(F32)
    codes = lax.dot_general(pick, weights.astype(BF16), NT, preferred_element_type=F32)
    place = jnp.where(codes[:1] == column_id, 1.0, 0.0).astype(BF16)
    others = jnp.sum(jnp.where(last, 0.0, weights), axis=1, keepdims=True)
    weights = jnp.where(last, float(marks) - others, weights)
    high, mid, low = (
        jnp.dot(place, y, preferred_element_type=F32)
        for y in split3(jnp.concatenate([values, weights], axis=1))
    )
    sums = high + (mid + low)
    background = background_ref[...].reshape(columns, num_levels)
    visc = jnp.exp((sums[:, :num_levels] + background) / (sums[:, num_levels:] + 1.0))
    visc = visc.reshape(cells_x, cells_y, num_levels)
    out_ref[...] = visc
    odd = here_ref[:1, :] % 2 == 1
    first, final = visc[:HALO], visc[cells_x - HALO :]
    near_ref[...] = jnp.where(odd, first, final)
    far_ref[...] = jnp.where(odd, final, first)


def gather(here, arrived, background, marks):
    strip = (HALO,) + background.shape[1:]
    return pl.pallas_call(
        functools.partial(gather_kernel, marks),
        out_shape=(
            jax.ShapeDtypeStruct(background.shape, F32),
            jax.ShapeDtypeStruct(strip, F32),
            jax.ShapeDtypeStruct(strip, F32),
        ),
        in_specs=[VMEM, VMEM, VMEM],
        out_specs=(VMEM, VMEM, VMEM),
        compiler_params=pltpu.CompilerParams(vmem_limit_bytes=48 << 20),
        name="gather",
    )(here, arrived, background)


def stokes_kernel(
    cells_y,
    sizes,
    here_ref,
    vel_ref,
    press_ref,
    buoy_ref,
    visc_ref,
    new_vel_ref,
    new_press_ref,
    visc_out_ref,
):
    wide_x, rows, num_levels = visc_ref.shape
    cells_x = wide_x - 2 * HALO
    row = lax.broadcasted_iota(jnp.int32, (rows, num_levels), 0)
    lane = lax.broadcasted_iota(jnp.int32, (rows, num_levels), 1)
    size_x, size_y = sizes[0] * cells_x, sizes[1] * cells_y
    first_x = jnp.broadcast_to(here_ref[:1, :], row.shape) * cells_x
    at_y = row + (here_ref[1:2, :] * cells_y - HALO)
    in_y = (at_y >= 0) & (at_y < size_y)
    in_y_face = (at_y >= 0) & (at_y < size_y - 1)
    low_lane = lane == 0
    high_lane = lane == num_levels - 1

    def north(f):
        return pltpu.roll(f, rows - 1, 0)

    def south(f):
        return pltpu.roll(f, 1, 0)

    def upper(f):
        return jnp.where(high_lane, 0.0, pltpu.roll(f, num_levels - 1, 1))

    def lower(f):
        return jnp.where(low_lane, 0.0, pltpu.roll(f, 1, 1))

    def in_x(x):
        at_x = first_x - HALO + x
        return (at_x >= 0) & (at_x < size_x)

    def in_x_face(x):
        at_x = first_x - HALO + x
        return (at_x >= 0) & (at_x < size_x - 1)

    inside = [in_y & in_x(x) for x in range(wide_x)]

    def known(ref, x, *lead):
        return jnp.where(inside[x], ref[(*lead, x)], 0.0)

    visc = [known(visc_ref, x) for x in range(wide_x)]
    vel = [[known(vel_ref, x, c) for x in range(wide_x)] for c in range(3)]
    press = [known(press_ref, x) for x in range(wide_x)]
    side_x = [visc[x] + visc[x + 1] for x in range(wide_x - 1)]
    side_y = [visc[x] + north(visc[x]) for x in range(wide_x)]
    side_z = [visc[x] + upper(visc[x]) for x in range(wide_x)]
    corner_xy = [0.25 * (side_y[x] + side_y[x + 1]) for x in range(wide_x - 1)]
    corner_xz = [0.25 * (side_x[x] + upper(side_x[x])) for x in range(wide_x - 1)]
    corner_yz = [0.25 * (side_y[x] + upper(side_y[x])) for x in range(wide_x)]
    rate_x = [(2.0 * VEL_STEP) / side for side in side_x]
    rate_y = [(2.0 * VEL_STEP) / side for side in side_y]
    rate_z = [(2.0 * VEL_STEP) / side for side in side_z]
    moment = [[None] * wide_x for _ in range(3)]
    for sweep in range(ITERS):
        begin, end = sweep, wide_x - sweep
        sig_x, sig_y, sig_z = {}, {}, {}
        tau_xy, tau_xz, tau_yz = {}, {}, {}
        for x in range(begin, end):
            u, v, w = vel[0][x], vel[1][x], vel[2][x]
            if x > begin:
                grad_x = u - vel[0][x - 1]
                grad_y = v - south(v)
                grad_z = w - lower(w)
                div = grad_x + grad_y + grad_z
                press[x] = press[x] - PRESS_STEP * visc[x] * div
                third = div / 3.0
                twice = 2.0 * visc[x]
                sig_x[x] = twice * (grad_x - third) - press[x]
                sig_y[x] = twice * (grad_y - third) - press[x]
                sig_z[x] = twice * (grad_z - third) - press[x]
                tau_yz[x] = jnp.where(
                    in_y, corner_yz[x] * (upper(v) - v + north(w) - w), 0.0
                )
            if x < end - 1:
                tau_xy[x] = jnp.where(
                    inside[x], corner_xy[x] * (north(u) - u + vel[1][x + 1] - v), 0.0
                )
                tau_xz[x] = jnp.where(
                    in_x(x), corner_xz[x] * (upper(u) - u + vel[2][x + 1] - w), 0.0
                )
        fresh = [[None] * wide_x for _ in range(3)]
        for x in range(begin + 1, end - 1):
            res_x = (
                sig_x[x + 1]
                - sig_x[x]
                + tau_xy[x]
                - south(tau_xy[x])
                + tau_xz[x]
                - lower(tau_xz[x])
            )
            res_y = (
                tau_xy[x]
                - tau_xy[x - 1]
                + north(sig_y[x])
                - sig_y[x]
                + tau_yz[x]
                - lower(tau_yz[x])
            )
            res_z = (
                tau_xz[x]
                - tau_xz[x - 1]
                + tau_yz[x]
                - south(tau_yz[x])
                + upper(sig_z[x])
                - sig_z[x]
                + buoy_ref[x]
            )
            masks = (
                in_y & in_x_face(x),
                in_y_face & in_x(x),
                (in_y & jnp.logical_not(high_lane)) & in_x(x),
            )
            for c, (res, rate, mask) in enumerate(
                zip((res_x, res_y, res_z), (rate_x, rate_y, rate_z), masks)
            ):
                if sweep > 0:
                    res = DAMPING * moment[c][x] + res
                moment[c][x] = res
                fresh[c][x] = jnp.where(mask, vel[c][x] + res * rate[x], 0.0)
        vel = fresh
    for x in range(cells_x):
        for c in range(3):
            new_vel_ref[c, x] = vel[c][x + HALO][HALO : HALO + cells_y]
        new_press_ref[x] = press[x + HALO][HALO : HALO + cells_y]
        visc_out_ref[x] = visc[x + HALO][HALO : HALO + cells_y]


def stokes(here, vel, press, buoy, visc, cells_y, sizes):
    wide_x, _, num_levels = visc.shape
    cells_x = wide_x - 2 * HALO
    return pl.pallas_call(
        functools.partial(stokes_kernel, cells_y, sizes),
        out_shape=(
            jax.ShapeDtypeStruct((3, cells_x, cells_y, num_levels), F32),
            jax.ShapeDtypeStruct((cells_x, cells_y, num_levels), F32),
            jax.ShapeDtypeStruct((cells_x, cells_y, num_levels), F32),
        ),
        in_specs=[VMEM] * 5,
        out_specs=(VMEM, VMEM, VMEM),
        compiler_params=pltpu.CompilerParams(vmem_limit_bytes=48 << 20),
        name="stokes",
    )(here, vel, press, buoy, visc)


def partners(size_x, size_y):
    def flat(x, y):
        return (x % size_x) * size_y + y

    cells = [(x, y) for x in range(size_x) for y in range(size_y)]
    x_near = [(flat(x, y), flat(x ^ 1, y)) for x, y in cells]
    x_far = [(flat(x, y), flat(x + 1 if x % 2 else x - 1, y)) for x, y in cells]
    y_near = [(flat(x, y), flat(x, y ^ 1)) for x, y in cells]
    y_far = [
        (flat(x, y), flat(x ^ 1, y) if y in (0, size_y - 1) else flat(x, y + 1 if y % 2 else y - 1))
        for x, y in cells
    ]
    return x_near, x_far, y_near, y_far


def swapped(near, far, near_pairs, far_pairs, odd, dim, x):
    near = lax.ppermute(near, ("gx", "gy"), near_pairs)
    far = lax.ppermute(far, ("gx", "gy"), far_pairs)
    before, after = jnp.where(odd, near, far), jnp.where(odd, far, near)
    return jnp.concatenate([before, x, after], axis=dim)


def strips(x, odd, dim):
    length = x.shape[dim]
    first = lax.slice_in_dim(x, 0, HALO, axis=dim)
    final = lax.slice_in_dim(x, length - HALO, length, axis=dim)
    return jnp.where(odd, first, final), jnp.where(odd, final, first)


def widened(x, near, far, pairs, odd_x, odd_y):
    dim = x.ndim - 3
    x = swapped(near, far, pairs[0], pairs[1], odd_x, dim, x)
    x = swapped(*strips(x, odd_y, dim + 1), pairs[2], pairs[3], odd_y, dim + 1, x)
    pad = jnp.zeros(x.shape[:-2] + (-x.shape[-2] % 8, x.shape[-1]), x.dtype)
    return jnp.concatenate([x, pad], axis=dim + 1)


def shards(
    velocity,
    pressure,
    buoyancy,
    background,
    marker_value,
    marker_height,
    marker_owner,
    marker_column,
    block_count,
):
    cells_x, cells_y, num_levels = pressure.shape
    block_rows, marks = marker_value.shape
    size_x = lax.axis_size("gx")
    size_y = lax.axis_size("gy")
    devices = size_x * size_y
    capacity = max(2, (2 * block_rows + devices - 1) // devices)
    send = deposit(
        block_count,
        marker_owner,
        marker_column,
        marker_value,
        marker_height,
        devices,
        capacity,
        num_levels,
    )
    arrived = lax.all_to_all(
        send.reshape(devices, capacity, 2 * num_levels),
        ("gx", "gy"),
        split_axis=0,
        concat_axis=0,
        tiled=True,
    ).reshape(devices * capacity, 2 * num_levels)
    pairs = partners(size_x, size_y)
    place_x, place_y = lax.axis_index("gx"), lax.axis_index("gy")
    odd_x, odd_y = place_x % 2, place_y % 2
    here = jnp.where(lax.broadcasted_iota(jnp.int32, (8, num_levels), 0) == 0, place_x, place_y)
    fields = jnp.concatenate([velocity, pressure[None], buoyancy[None]], axis=0)
    fields = widened(fields, *strips(fields, odd_x == 1, 1), pairs, odd_x == 1, odd_y == 1)
    visc, near, far = gather(here, arrived, background, marks)
    visc = widened(visc, near, far, pairs, odd_x == 1, odd_y == 1)
    return stokes(
        here, fields[:3], fields[3], fields[4], visc, cells_y, (size_x, size_y)
    )


def solution(mesh):
    return jax.shard_map(
        shards,
        mesh=mesh,
        in_specs=(
            P(None, "gx", "gy", None),
            P("gx", "gy", None),
            P("gx", "gy", None),
            P("gx", "gy", None),
            P(("gx", "gy"), None),
            P(("gx", "gy"), None),
            P(("gx", "gy"), None),
            P(("gx", "gy")),
            P(("gx", "gy")),
        ),
        out_specs=(P(None, "gx", "gy", None), P("gx", "gy", None), P("gx", "gy", None)),
        check_vma=False,
    )
```

```python
import functools

import jax
import jax.numpy as jnp
from jax import lax
from jax.experimental import pallas as pl
from jax.experimental.pallas import tpu as pltpu
from jax.sharding import PartitionSpec as P

ITERS = 2
HALO = 2
WAYS = 4
OUT_PARTS = 4

PRESS_STEP = 0.5
VEL_STEP = 0.05
DAMPING = 0.8

F32 = jnp.float32
BF16 = jnp.bfloat16
VMEM = pl.BlockSpec(memory_space=pltpu.VMEM)
HBM = pl.BlockSpec(memory_space=pltpu.HBM)
SMEM = pl.BlockSpec(memory_space=pltpu.SMEM)
NT = (((1,), (1,)), ((), ()))


def split3(x):
    high = x.astype(BF16)
    rest = x - high.astype(F32)
    mid = rest.astype(BF16)
    low = (rest - mid.astype(F32)).astype(BF16)
    return high, mid, low


def deposit_kernel(
    num_owners,
    capacity,
    count_ref,
    owner_hbm,
    column_hbm,
    value_hbm,
    height_hbm,
    out_hbm,
    value_ref,
    height_ref,
    owner_ref,
    column_ref,
    place_ref,
    code_ref,
    lower_ref,
    fraction_ref,
    part_ref,
    out_ref,
    sem,
    out_sem,
):
    blocks, marks = value_ref.shape
    num_levels = out_ref.shape[1] // 2
    slots = num_owners * capacity

    copies = (
        pltpu.make_async_copy(owner_hbm, owner_ref, sem.at[0]),
        pltpu.make_async_copy(column_hbm, column_ref, sem.at[1]),
        pltpu.make_async_copy(height_hbm, height_ref, sem.at[2]),
        pltpu.make_async_copy(value_hbm, value_ref, sem.at[3]),
    )
    for copy in copies:
        copy.start()
    for copy in copies:
        copy.wait()

    owner = owner_ref[...]
    block_id = lax.broadcasted_iota(jnp.int32, (1, blocks), 1)
    owner = jnp.where(block_id < count_ref[0], owner, num_owners)
    owned = lax.broadcasted_iota(jnp.int32, (num_owners, blocks), 0) == owner
    hits = jnp.where(owned, 1.0, 0.0)
    earlier = jnp.where(
        lax.broadcasted_iota(jnp.int32, (blocks, blocks), 0)
        < lax.broadcasted_iota(jnp.int32, (blocks, blocks), 1),
        1.0,
        0.0,
    ).astype(BF16)
    before = jnp.dot(hits.astype(BF16), earlier, preferred_element_type=F32)
    rank = jnp.sum(hits * before, axis=0, keepdims=True)
    slot = owner * capacity + rank.astype(jnp.int32)
    place = jnp.where(
        lax.broadcasted_iota(jnp.int32, (slots, blocks), 0) == slot, 1.0, 0.0
    ).astype(BF16)
    place_ref[...] = place
    code = jnp.broadcast_to((column_ref[...] + 1).astype(F32), (num_levels, blocks)).astype(BF16)
    code_ref[...] = lax.dot_general(place, code, NT, preferred_element_type=F32)

    span = num_levels // WAYS
    row8 = lax.broadcasted_iota(jnp.int32, (8, marks), 0)
    upper_part = (row8 & 1) == 1
    with_value = (row8 & 2) == 0
    leading = row8 < 4
    offset_id = lax.broadcasted_iota(jnp.int32, (span, marks), 0).astype(F32).astype(BF16)
    lane_window = lax.broadcasted_iota(jnp.int32, (8, num_levels), 1) // span

    def operands(b):
        lower = jnp.broadcast_to(lower_ref[pl.ds(b, 1), :], (8, marks))
        fraction = jnp.broadcast_to(fraction_ref[pl.ds(b, 1), :], (8, marks))
        value = jnp.broadcast_to(value_ref[pl.ds(b, 1), :], (8, marks))
        share = jnp.where(upper_part, fraction, 1.0 - fraction)
        share = share * jnp.where(with_value, value, 1.0)
        high = share.astype(BF16).astype(F32)
        pieces = jnp.where(leading, high, share - high)
        window = jnp.floor(lower * (1.0 / span))
        offset = lower - window * span
        offset = jnp.concatenate([offset, offset], axis=0).astype(BF16)
        offset = jnp.concatenate([offset] * (span // 16), axis=0)
        hot = jnp.where(offset == offset_id, jnp.ones((), BF16), jnp.zeros((), BF16))
        return [jnp.where(window == a, pieces, 0.0) for a in range(WAYS)], hot

    height = height_ref[...]
    lower = jnp.minimum(jnp.floor(height), num_levels - 2.0)
    lower_ref[...] = lower
    fraction_ref[...] = height - lower
    for b in range(0, blocks, WAYS):
        pieces, hots = zip(*(operands(b + i) for i in range(WAYS)))
        sums = lax.dot_general(
            jnp.concatenate(sum(pieces, []), axis=0).astype(BF16),
            jnp.concatenate(hots, axis=0),
            NT,
            preferred_element_type=F32,
        )
        for i in range(WAYS):
            total = jnp.zeros((8, num_levels), F32)
            for a in range(WAYS):
                found = sums[(i * WAYS + a) * 8 : (i * WAYS + a + 1) * 8]
                turn = ((a - i) * span) % num_levels
                found = pltpu.roll(found, turn, 1) if turn else found
                total = jnp.where(lane_window == a, found, total)
            part_ref[(b + i) * 8 : (b + i + 1) * 8, :] = total

    def part(kind):
        high = part_ref[pl.ds(kind, blocks, stride=8), :]
        return high + part_ref[pl.ds(kind + 4, blocks, stride=8), :]

    value_sum = part(0) + pltpu.roll(part(1), 1, 1)
    weight_sum = part(2) + pltpu.roll(part(3), 1, 1)
    pieces = split3(jnp.concatenate([value_sum, weight_sum], axis=1))
    size = slots // OUT_PARTS
    copies = []
    for p in range(OUT_PARTS):
        rows = slice(p * size, (p + 1) * size)
        high, mid, low = (
            jnp.dot(place_ref[rows], y, preferred_element_type=F32) for y in pieces
        )
        sums = high + (mid + low)
        lane = lax.broadcasted_iota(jnp.int32, (size, num_levels), 1)
        out_ref[rows, :num_levels] = sums[:, :num_levels]
        out_ref[rows, num_levels:] = jnp.where(
            lane == num_levels - 1, code_ref[rows], sums[:, num_levels:]
        )
        copy = pltpu.make_async_copy(out_ref.at[rows], out_hbm.at[rows], out_sem.at[p])
        copy.start()
        copies.append(copy)
    for copy in copies:
        copy.wait()


def deposit(count, owner, column, value, height, num_owners, capacity, num_levels):
    blocks, marks = value.shape
    slots = num_owners * capacity
    return pl.pallas_call(
        functools.partial(deposit_kernel, num_owners, capacity),
        out_shape=jax.ShapeDtypeStruct((slots, 2 * num_levels), F32),
        in_specs=[SMEM, HBM, HBM, HBM, HBM],
        out_specs=HBM,
        scratch_shapes=[
            pltpu.VMEM((blocks, marks), F32),
            pltpu.VMEM((blocks, marks), F32),
            pltpu.VMEM((1, blocks), jnp.int32),
            pltpu.VMEM((1, blocks), jnp.int32),
            pltpu.VMEM((slots, blocks), BF16),
            pltpu.VMEM((slots, num_levels), F32),
            pltpu.VMEM((blocks, marks), F32),
            pltpu.VMEM((blocks, marks), F32),
            pltpu.VMEM((blocks * 8, num_levels), F32),
            pltpu.VMEM((slots, 2 * num_levels), F32),
            pltpu.SemaphoreType.DMA((4,)),
            pltpu.SemaphoreType.DMA((OUT_PARTS,)),
        ],
        compiler_params=pltpu.CompilerParams(vmem_limit_bytes=60 << 20),
        name="deposit",
    )(count, owner.reshape(1, blocks), column.reshape(1, blocks), value, height)


def gather_kernel(marks, here_ref, arrived_ref, background_ref, out_ref, near_ref, far_ref):
    slots = arrived_ref.shape[0]
    cells_x, cells_y, num_levels = out_ref.shape
    columns = cells_x * cells_y
    values = arrived_ref[:, :num_levels]
    weights = arrived_ref[:, num_levels:]
    last = lax.broadcasted_iota(jnp.int32, (slots, num_levels), 1) == num_levels - 1
    pick = jnp.where(
        lax.broadcasted_iota(jnp.int32, (8, num_levels), 1) == num_levels - 1, 1.0, 0.0
    ).astype(BF16)
    column_id = (lax.broadcasted_iota(jnp.int32, (columns, slots), 0) + 1).astype(F32)
    codes = lax.dot_general(pick, weights.astype(BF16), NT, preferred_element_type=F32)
    place = jnp.where(codes[:1] == column_id, 1.0, 0.0).astype(BF16)
    others = jnp.sum(jnp.where(last, 0.0, weights), axis=1, keepdims=True)
    weights = jnp.where(last, float(marks) - others, weights)
    high, mid, low = (
        jnp.dot(place, y, preferred_element_type=F32)
        for y in split3(jnp.concatenate([values, weights], axis=1))
    )
    sums = high + (mid + low)
    background = background_ref[...].reshape(columns, num_levels)
    visc = jnp.exp((sums[:, :num_levels] + background) / (sums[:, num_levels:] + 1.0))
    visc = visc.reshape(cells_x, cells_y, num_levels)
    out_ref[...] = visc
    odd = here_ref[:1, :] % 2 == 1
    first, final = visc[:HALO], visc[cells_x - HALO :]
    near_ref[...] = jnp.where(odd, first, final)
    far_ref[...] = jnp.where(odd, final, first)


def gather(here, arrived, background, marks):
    strip = (HALO,) + background.shape[1:]
    return pl.pallas_call(
        functools.partial(gather_kernel, marks),
        out_shape=(
            jax.ShapeDtypeStruct(background.shape, F32),
            jax.ShapeDtypeStruct(strip, F32),
            jax.ShapeDtypeStruct(strip, F32),
        ),
        in_specs=[VMEM, VMEM, VMEM],
        out_specs=(VMEM, VMEM, VMEM),
        compiler_params=pltpu.CompilerParams(vmem_limit_bytes=48 << 20),
        name="gather",
    )(here, arrived, background)


def stokes_kernel(
    cells_y,
    sizes,
    here_ref,
    vel_ref,
    press_ref,
    buoy_ref,
    visc_ref,
    new_vel_ref,
    new_press_ref,
    visc_out_ref,
):
    wide_x, rows, num_levels = visc_ref.shape
    cells_x = wide_x - 2 * HALO
    row = lax.broadcasted_iota(jnp.int32, (rows, num_levels), 0)
    lane = lax.broadcasted_iota(jnp.int32, (rows, num_levels), 1)
    size_x, size_y = sizes[0] * cells_x, sizes[1] * cells_y
    first_x = jnp.broadcast_to(here_ref[:1, :], row.shape) * cells_x
    at_y = row + (here_ref[1:2, :] * cells_y - HALO)
    in_y = (at_y >= 0) & (at_y < size_y)
    in_y_face = (at_y >= 0) & (at_y < size_y - 1)
    low_lane = lane == 0
    high_lane = lane == num_levels - 1

    def north(f):
        return pltpu.roll(f, rows - 1, 0)

    def south(f):
        return pltpu.roll(f, 1, 0)

    def upper(f):
        return jnp.where(high_lane, 0.0, pltpu.roll(f, num_levels - 1, 1))

    def lower(f):
        return jnp.where(low_lane, 0.0, pltpu.roll(f, 1, 1))

    def in_x(x):
        at_x = first_x - HALO + x
        return (at_x >= 0) & (at_x < size_x)

    def in_x_face(x):
        at_x = first_x - HALO + x
        return (at_x >= 0) & (at_x < size_x - 1)

    inside = [in_y & in_x(x) for x in range(wide_x)]

    def known(ref, x, *lead):
        return jnp.where(inside[x], ref[(*lead, x)], 0.0)

    visc = [known(visc_ref, x) for x in range(wide_x)]
    vel = [[known(vel_ref, x, c) for x in range(wide_x)] for c in range(3)]
    press = [known(press_ref, x) for x in range(wide_x)]
    side_x = [visc[x] + visc[x + 1] for x in range(wide_x - 1)]
    side_y = [visc[x] + north(visc[x]) for x in range(wide_x)]
    side_z = [visc[x] + upper(visc[x]) for x in range(wide_x)]
    corner_xy = [0.25 * (side_y[x] + side_y[x + 1]) for x in range(wide_x - 1)]
    corner_xz = [0.25 * (side_x[x] + upper(side_x[x])) for x in range(wide_x - 1)]
    corner_yz = [0.25 * (side_y[x] + upper(side_y[x])) for x in range(wide_x)]
    rate_x = [(2.0 * VEL_STEP) / side for side in side_x]
    rate_y = [(2.0 * VEL_STEP) / side for side in side_y]
    rate_z = [(2.0 * VEL_STEP) / side for side in side_z]
    moment = [[None] * wide_x for _ in range(3)]
    for sweep in range(ITERS):
        begin, end = sweep, wide_x - sweep
        sig_x, sig_y, sig_z = {}, {}, {}
        tau_xy, tau_xz, tau_yz = {}, {}, {}
        for x in range(begin, end):
            u, v, w = vel[0][x], vel[1][x], vel[2][x]
            if x > begin:
                grad_x = u - vel[0][x - 1]
                grad_y = v - south(v)
                grad_z = w - lower(w)
                div = grad_x + grad_y + grad_z
                press[x] = press[x] - PRESS_STEP * visc[x] * div
                third = div / 3.0
                twice = 2.0 * visc[x]
                sig_x[x] = twice * (grad_x - third) - press[x]
                sig_y[x] = twice * (grad_y - third) - press[x]
                sig_z[x] = twice * (grad_z - third) - press[x]
                tau_yz[x] = jnp.where(
                    in_y, corner_yz[x] * (upper(v) - v + north(w) - w), 0.0
                )
            if x < end - 1:
                tau_xy[x] = jnp.where(
                    inside[x], corner_xy[x] * (north(u) - u + vel[1][x + 1] - v), 0.0
                )
                tau_xz[x] = jnp.where(
                    in_x(x), corner_xz[x] * (upper(u) - u + vel[2][x + 1] - w), 0.0
                )
        fresh = [[None] * wide_x for _ in range(3)]
        for x in range(begin + 1, end - 1):
            res_x = (
                sig_x[x + 1]
                - sig_x[x]
                + tau_xy[x]
                - south(tau_xy[x])
                + tau_xz[x]
                - lower(tau_xz[x])
            )
            res_y = (
                tau_xy[x]
                - tau_xy[x - 1]
                + north(sig_y[x])
                - sig_y[x]
                + tau_yz[x]
                - lower(tau_yz[x])
            )
            res_z = (
                tau_xz[x]
                - tau_xz[x - 1]
                + tau_yz[x]
                - south(tau_yz[x])
                + upper(sig_z[x])
                - sig_z[x]
                + buoy_ref[x]
            )
            masks = (
                in_y & in_x_face(x),
                in_y_face & in_x(x),
                (in_y & jnp.logical_not(high_lane)) & in_x(x),
            )
            for c, (res, rate, mask) in enumerate(
                zip((res_x, res_y, res_z), (rate_x, rate_y, rate_z), masks)
            ):
                if sweep > 0:
                    res = DAMPING * moment[c][x] + res
                moment[c][x] = res
                fresh[c][x] = jnp.where(mask, vel[c][x] + res * rate[x], 0.0)
        vel = fresh
    for x in range(cells_x):
        for c in range(3):
            new_vel_ref[c, x] = vel[c][x + HALO][HALO : HALO + cells_y]
        new_press_ref[x] = press[x + HALO][HALO : HALO + cells_y]
        visc_out_ref[x] = visc[x + HALO][HALO : HALO + cells_y]


def stokes(here, vel, press, buoy, visc, cells_y, sizes):
    wide_x, _, num_levels = visc.shape
    cells_x = wide_x - 2 * HALO
    return pl.pallas_call(
        functools.partial(stokes_kernel, cells_y, sizes),
        out_shape=(
            jax.ShapeDtypeStruct((3, cells_x, cells_y, num_levels), F32),
            jax.ShapeDtypeStruct((cells_x, cells_y, num_levels), F32),
            jax.ShapeDtypeStruct((cells_x, cells_y, num_levels), F32),
        ),
        in_specs=[VMEM] * 5,
        out_specs=(VMEM, VMEM, VMEM),
        compiler_params=pltpu.CompilerParams(vmem_limit_bytes=48 << 20),
        name="stokes",
    )(here, vel, press, buoy, visc)


def partners(size_x, size_y):
    def flat(x, y):
        return (x % size_x) * size_y + y

    cells = [(x, y) for x in range(size_x) for y in range(size_y)]
    x_near = [(flat(x, y), flat(x ^ 1, y)) for x, y in cells]
    x_far = [(flat(x, y), flat(x + 1 if x % 2 else x - 1, y)) for x, y in cells]
    y_near = [(flat(x, y), flat(x, y ^ 1)) for x, y in cells]
    y_far = [
        (flat(x, y), flat(x ^ 1, y) if y in (0, size_y - 1) else flat(x, y + 1 if y % 2 else y - 1))
        for x, y in cells
    ]
    return x_near, x_far, y_near, y_far


def swapped(near, far, near_pairs, far_pairs, odd, dim, x):
    near = lax.ppermute(near, ("gx", "gy"), near_pairs)
    far = lax.ppermute(far, ("gx", "gy"), far_pairs)
    before, after = jnp.where(odd, near, far), jnp.where(odd, far, near)
    return jnp.concatenate([before, x, after], axis=dim)


def strips(x, odd, dim):
    length = x.shape[dim]
    first = lax.slice_in_dim(x, 0, HALO, axis=dim)
    final = lax.slice_in_dim(x, length - HALO, length, axis=dim)
    return jnp.where(odd, first, final), jnp.where(odd, final, first)


def widened(x, near, far, pairs, odd_x, odd_y):
    dim = x.ndim - 3
    x = swapped(near, far, pairs[0], pairs[1], odd_x, dim, x)
    x = swapped(*strips(x, odd_y, dim + 1), pairs[2], pairs[3], odd_y, dim + 1, x)
    pad = jnp.zeros(x.shape[:-2] + (-x.shape[-2] % 8, x.shape[-1]), x.dtype)
    return jnp.concatenate([x, pad], axis=dim + 1)


def shards(
    velocity,
    pressure,
    buoyancy,
    background,
    marker_value,
    marker_height,
    marker_owner,
    marker_column,
    block_count,
):
    cells_x, cells_y, num_levels = pressure.shape
    block_rows, marks = marker_value.shape
    size_x = lax.axis_size("gx")
    size_y = lax.axis_size("gy")
    devices = size_x * size_y
    capacity = max(2, (2 * block_rows + devices - 1) // devices)
    send = deposit(
        block_count,
        marker_owner,
        marker_column,
        marker_value,
        marker_height,
        devices,
        capacity,
        num_levels,
    )
    arrived = lax.all_to_all(
        send.reshape(devices, capacity, 2 * num_levels),
        ("gx", "gy"),
        split_axis=0,
        concat_axis=0,
        tiled=True,
    ).reshape(devices * capacity, 2 * num_levels)
    pairs = partners(size_x, size_y)
    place_x, place_y = lax.axis_index("gx"), lax.axis_index("gy")
    odd_x, odd_y = place_x % 2, place_y % 2
    here = jnp.where(lax.broadcasted_iota(jnp.int32, (8, num_levels), 0) == 0, place_x, place_y)
    fields = jnp.concatenate([velocity, pressure[None], buoyancy[None]], axis=0)
    near, far = strips(fields, odd_x == 1, 1)
    near, here = lax.optimization_barrier((near, here))
    fields = widened(fields, near, far, pairs, odd_x == 1, odd_y == 1)
    visc, near, far = gather(here, arrived, background, marks)
    visc = widened(visc, near, far, pairs, odd_x == 1, odd_y == 1)
    return stokes(
        here, fields[:3], fields[3], fields[4], visc, cells_y, (size_x, size_y)
    )


def solution(mesh):
    return jax.shard_map(
        shards,
        mesh=mesh,
        in_specs=(
            P(None, "gx", "gy", None),
            P("gx", "gy", None),
            P("gx", "gy", None),
            P("gx", "gy", None),
            P(("gx", "gy"), None),
            P(("gx", "gy"), None),
            P(("gx", "gy"), None),
            P(("gx", "gy")),
            P(("gx", "gy")),
        ),
        out_specs=(P(None, "gx", "gy", None), P("gx", "gy", None), P("gx", "gy", None)),
        check_vma=False,
    )
```

```python
import functools

import jax
import jax.numpy as jnp
from jax import lax
from jax.experimental import pallas as pl
from jax.experimental.pallas import tpu as pltpu
from jax.sharding import PartitionSpec as P

ITERS = 2
HALO = 2
WAYS = 4
OUT_PARTS = 4

PRESS_STEP = 0.5
VEL_STEP = 0.05
DAMPING = 0.8

F32 = jnp.float32
BF16 = jnp.bfloat16
VMEM = pl.BlockSpec(memory_space=pltpu.VMEM)
HBM = pl.BlockSpec(memory_space=pltpu.HBM)
SMEM = pl.BlockSpec(memory_space=pltpu.SMEM)
NT = (((1,), (1,)), ((), ()))


def split3(x):
    high = x.astype(BF16)
    rest = x - high.astype(F32)
    mid = rest.astype(BF16)
    low = (rest - mid.astype(F32)).astype(BF16)
    return high, mid, low


def deposit_kernel(
    num_owners,
    capacity,
    count_ref,
    owner_hbm,
    column_hbm,
    value_hbm,
    height_hbm,
    out_hbm,
    value_ref,
    height_ref,
    owner_ref,
    column_ref,
    place_ref,
    code_ref,
    lower_ref,
    fraction_ref,
    part_ref,
    out_ref,
    sem,
    out_sem,
):
    blocks, marks = value_ref.shape
    num_levels = out_ref.shape[1] // 2
    slots = num_owners * capacity

    copies = (
        pltpu.make_async_copy(owner_hbm, owner_ref, sem.at[0]),
        pltpu.make_async_copy(column_hbm, column_ref, sem.at[1]),
        pltpu.make_async_copy(height_hbm, height_ref, sem.at[2]),
        pltpu.make_async_copy(value_hbm, value_ref, sem.at[3]),
    )
    for copy in copies:
        copy.start()
    for copy in copies:
        copy.wait()

    owner = owner_ref[...]
    block_id = lax.broadcasted_iota(jnp.int32, (1, blocks), 1)
    owner = jnp.where(block_id < count_ref[0], owner, num_owners)
    owned = lax.broadcasted_iota(jnp.int32, (num_owners, blocks), 0) == owner
    hits = jnp.where(owned, 1.0, 0.0)
    earlier = jnp.where(
        lax.broadcasted_iota(jnp.int32, (blocks, blocks), 0)
        < lax.broadcasted_iota(jnp.int32, (blocks, blocks), 1),
        1.0,
        0.0,
    ).astype(BF16)
    before = jnp.dot(hits.astype(BF16), earlier, preferred_element_type=F32)
    rank = jnp.sum(hits * before, axis=0, keepdims=True)
    slot = owner * capacity + rank.astype(jnp.int32)
    place = jnp.where(
        lax.broadcasted_iota(jnp.int32, (slots, blocks), 0) == slot, 1.0, 0.0
    ).astype(BF16)
    place_ref[...] = place
    code = jnp.broadcast_to((column_ref[...] + 1).astype(F32), (num_levels, blocks)).astype(BF16)
    code_ref[...] = lax.dot_general(place, code, NT, preferred_element_type=F32)

    span = num_levels // WAYS
    row8 = lax.broadcasted_iota(jnp.int32, (8, marks), 0)
    upper_part = (row8 & 1) == 1
    with_value = (row8 & 2) == 0
    leading = row8 < 4
    offset_id = lax.broadcasted_iota(jnp.int32, (span, marks), 0).astype(F32).astype(BF16)
    lane_window = lax.broadcasted_iota(jnp.int32, (8, num_levels), 1) // span

    def operands(b):
        lower = jnp.broadcast_to(lower_ref[pl.ds(b, 1), :], (8, marks))
        fraction = jnp.broadcast_to(fraction_ref[pl.ds(b, 1), :], (8, marks))
        value = jnp.broadcast_to(value_ref[pl.ds(b, 1), :], (8, marks))
        share = jnp.where(upper_part, fraction, 1.0 - fraction)
        share = share * jnp.where(with_value, value, 1.0)
        high = share.astype(BF16).astype(F32)
        pieces = jnp.where(leading, high, share - high)
        window = jnp.floor(lower * (1.0 / span))
        offset = lower - window * span
        offset = jnp.concatenate([offset, offset], axis=0).astype(BF16)
        offset = jnp.concatenate([offset] * (span // 16), axis=0)
        hot = jnp.where(offset == offset_id, jnp.ones((), BF16), jnp.zeros((), BF16))
        return [jnp.where(window == a, pieces, 0.0) for a in range(WAYS)], hot

    height = height_ref[...]
    lower = jnp.minimum(jnp.floor(height), num_levels - 2.0)
    lower_ref[...] = lower
    fraction_ref[...] = height - lower
    for b in range(0, blocks, WAYS):
        pieces, hots = zip(*(operands(b + i) for i in range(WAYS)))
        sums = lax.dot_general(
            jnp.concatenate(sum(pieces, []), axis=0).astype(BF16),
            jnp.concatenate(hots, axis=0),
            NT,
            preferred_element_type=F32,
        )
        for i in range(WAYS):
            total = jnp.zeros((8, num_levels), F32)
            for a in range(WAYS):
                found = sums[(i * WAYS + a) * 8 : (i * WAYS + a + 1) * 8]
                turn = ((a - i) * span) % num_levels
                found = pltpu.roll(found, turn, 1) if turn else found
                total = jnp.where(lane_window == a, found, total)
            part_ref[(b + i) * 8 : (b + i + 1) * 8, :] = total

    def part(kind):
        high = part_ref[pl.ds(kind, blocks, stride=8), :]
        return high + part_ref[pl.ds(kind + 4, blocks, stride=8), :]

    value_sum = part(0) + pltpu.roll(part(1), 1, 1)
    weight_sum = part(2) + pltpu.roll(part(3), 1, 1)
    pieces = split3(jnp.concatenate([value_sum, weight_sum], axis=1))
    size = slots // OUT_PARTS
    copies = []
    for p in range(OUT_PARTS):
        rows = slice(p * size, (p + 1) * size)
        high, mid, low = (
            jnp.dot(place_ref[rows], y, preferred_element_type=F32) for y in pieces
        )
        sums = high + (mid + low)
        lane = lax.broadcasted_iota(jnp.int32, (size, num_levels), 1)
        out_ref[rows, :num_levels] = sums[:, :num_levels]
        out_ref[rows, num_levels:] = jnp.where(
            lane == num_levels - 1, code_ref[rows], sums[:, num_levels:]
        )
        copy = pltpu.make_async_copy(out_ref.at[rows], out_hbm.at[rows], out_sem.at[p])
        copy.start()
        copies.append(copy)
    for copy in copies:
        copy.wait()


def deposit(count, owner, column, value, height, num_owners, capacity, num_levels):
    blocks, marks = value.shape
    slots = num_owners * capacity
    return pl.pallas_call(
        functools.partial(deposit_kernel, num_owners, capacity),
        out_shape=jax.ShapeDtypeStruct((slots, 2 * num_levels), F32),
        in_specs=[SMEM, HBM, HBM, HBM, HBM],
        out_specs=HBM,
        scratch_shapes=[
            pltpu.VMEM((blocks, marks), F32),
            pltpu.VMEM((blocks, marks), F32),
            pltpu.VMEM((1, blocks), jnp.int32),
            pltpu.VMEM((1, blocks), jnp.int32),
            pltpu.VMEM((slots, blocks), BF16),
            pltpu.VMEM((slots, num_levels), F32),
            pltpu.VMEM((blocks, marks), F32),
            pltpu.VMEM((blocks, marks), F32),
            pltpu.VMEM((blocks * 8 + 8, num_levels), F32),
            pltpu.VMEM((slots, 2 * num_levels), F32),
            pltpu.SemaphoreType.DMA((4,)),
            pltpu.SemaphoreType.DMA((OUT_PARTS,)),
        ],
        compiler_params=pltpu.CompilerParams(vmem_limit_bytes=60 << 20),
        name="deposit",
    )(count, owner.reshape(1, blocks), column.reshape(1, blocks), value, height)


def gather_kernel(marks, here_ref, arrived_ref, background_ref, out_ref, near_ref, far_ref):
    slots = arrived_ref.shape[0]
    cells_x, cells_y, num_levels = out_ref.shape
    columns = cells_x * cells_y
    values = arrived_ref[:, :num_levels]
    weights = arrived_ref[:, num_levels:]
    last = lax.broadcasted_iota(jnp.int32, (slots, num_levels), 1) == num_levels - 1
    pick = jnp.where(
        lax.broadcasted_iota(jnp.int32, (8, num_levels), 1) == num_levels - 1, 1.0, 0.0
    ).astype(BF16)
    column_id = (lax.broadcasted_iota(jnp.int32, (columns, slots), 0) + 1).astype(F32)
    codes = lax.dot_general(pick, weights.astype(BF16), NT, preferred_element_type=F32)
    place = jnp.where(codes[:1] == column_id, 1.0, 0.0).astype(BF16)
    others = jnp.sum(jnp.where(last, 0.0, weights), axis=1, keepdims=True)
    weights = jnp.where(last, float(marks) - others, weights)
    high, mid, low = (
        jnp.dot(place, y, preferred_element_type=F32)
        for y in split3(jnp.concatenate([values, weights], axis=1))
    )
    sums = high + (mid + low)
    background = background_ref[...].reshape(columns, num_levels)
    visc = jnp.exp((sums[:, :num_levels] + background) / (sums[:, num_levels:] + 1.0))
    visc = visc.reshape(cells_x, cells_y, num_levels)
    out_ref[...] = visc
    odd = here_ref[:1, :] % 2 == 1
    first, final = visc[:HALO], visc[cells_x - HALO :]
    near_ref[...] = jnp.where(odd, first, final)
    far_ref[...] = jnp.where(odd, final, first)


def gather(here, arrived, background, marks):
    strip = (HALO,) + background.shape[1:]
    return pl.pallas_call(
        functools.partial(gather_kernel, marks),
        out_shape=(
            jax.ShapeDtypeStruct(background.shape, F32),
            jax.ShapeDtypeStruct(strip, F32),
            jax.ShapeDtypeStruct(strip, F32),
        ),
        in_specs=[VMEM, VMEM, VMEM],
        out_specs=(VMEM, VMEM, VMEM),
        compiler_params=pltpu.CompilerParams(vmem_limit_bytes=48 << 20),
        name="gather",
    )(here, arrived, background)


def stokes_kernel(
    cells_y,
    sizes,
    here_ref,
    vel_ref,
    press_ref,
    buoy_ref,
    visc_ref,
    new_vel_ref,
    new_press_ref,
    visc_out_ref,
):
    wide_x, rows, num_levels = visc_ref.shape
    cells_x = wide_x - 2 * HALO
    row = lax.broadcasted_iota(jnp.int32, (rows, num_levels), 0)
    lane = lax.broadcasted_iota(jnp.int32, (rows, num_levels), 1)
    size_x, size_y = sizes[0] * cells_x, sizes[1] * cells_y
    first_x = jnp.broadcast_to(here_ref[:1, :], row.shape) * cells_x
    at_y = row + (here_ref[1:2, :] * cells_y - HALO)
    in_y = (at_y >= 0) & (at_y < size_y)
    in_y_face = (at_y >= 0) & (at_y < size_y - 1)
    low_lane = lane == 0
    high_lane = lane == num_levels - 1

    def north(f):
        return pltpu.roll(f, rows - 1, 0)

    def south(f):
        return pltpu.roll(f, 1, 0)

    def upper(f):
        return jnp.where(high_lane, 0.0, pltpu.roll(f, num_levels - 1, 1))

    def lower(f):
        return jnp.where(low_lane, 0.0, pltpu.roll(f, 1, 1))

    def in_x(x):
        at_x = first_x - HALO + x
        return (at_x >= 0) & (at_x < size_x)

    def in_x_face(x):
        at_x = first_x - HALO + x
        return (at_x >= 0) & (at_x < size_x - 1)

    inside = [in_y & in_x(x) for x in range(wide_x)]

    def known(ref, x, *lead):
        return jnp.where(inside[x], ref[(*lead, x)], 0.0)

    visc = [known(visc_ref, x) for x in range(wide_x)]
    vel = [[known(vel_ref, x, c) for x in range(wide_x)] for c in range(3)]
    press = [known(press_ref, x) for x in range(wide_x)]
    side_x = [visc[x] + visc[x + 1] for x in range(wide_x - 1)]
    side_y = [visc[x] + north(visc[x]) for x in range(wide_x)]
    side_z = [visc[x] + upper(visc[x]) for x in range(wide_x)]
    corner_xy = [0.25 * (side_y[x] + side_y[x + 1]) for x in range(wide_x - 1)]
    corner_xz = [0.25 * (side_x[x] + upper(side_x[x])) for x in range(wide_x - 1)]
    corner_yz = [0.25 * (side_y[x] + upper(side_y[x])) for x in range(wide_x)]
    rate_x = [(2.0 * VEL_STEP) / side for side in side_x]
    rate_y = [(2.0 * VEL_STEP) / side for side in side_y]
    rate_z = [(2.0 * VEL_STEP) / side for side in side_z]
    moment = [[None] * wide_x for _ in range(3)]
    for sweep in range(ITERS):
        begin, end = sweep, wide_x - sweep
        sig_x, sig_y, sig_z = {}, {}, {}
        tau_xy, tau_xz, tau_yz = {}, {}, {}
        for x in range(begin, end):
            u, v, w = vel[0][x], vel[1][x], vel[2][x]
            if x > begin:
                grad_x = u - vel[0][x - 1]
                grad_y = v - south(v)
                grad_z = w - lower(w)
                div = grad_x + grad_y + grad_z
                press[x] = press[x] - PRESS_STEP * visc[x] * div
                third = div / 3.0
                twice = 2.0 * visc[x]
                sig_x[x] = twice * (grad_x - third) - press[x]
                sig_y[x] = twice * (grad_y - third) - press[x]
                sig_z[x] = twice * (grad_z - third) - press[x]
                tau_yz[x] = jnp.where(
                    in_y, corner_yz[x] * (upper(v) - v + north(w) - w), 0.0
                )
            if x < end - 1:
                tau_xy[x] = jnp.where(
                    inside[x], corner_xy[x] * (north(u) - u + vel[1][x + 1] - v), 0.0
                )
                tau_xz[x] = jnp.where(
                    in_x(x), corner_xz[x] * (upper(u) - u + vel[2][x + 1] - w), 0.0
                )
        fresh = [[None] * wide_x for _ in range(3)]
        for x in range(begin + 1, end - 1):
            res_x = (
                sig_x[x + 1]
                - sig_x[x]
                + tau_xy[x]
                - south(tau_xy[x])
                + tau_xz[x]
                - lower(tau_xz[x])
            )
            res_y = (
                tau_xy[x]
                - tau_xy[x - 1]
                + north(sig_y[x])
                - sig_y[x]
                + tau_yz[x]
                - lower(tau_yz[x])
            )
            res_z = (
                tau_xz[x]
                - tau_xz[x - 1]
                + tau_yz[x]
                - south(tau_yz[x])
                + upper(sig_z[x])
                - sig_z[x]
                + buoy_ref[x]
            )
            masks = (
                in_y & in_x_face(x),
                in_y_face & in_x(x),
                (in_y & jnp.logical_not(high_lane)) & in_x(x),
            )
            for c, (res, rate, mask) in enumerate(
                zip((res_x, res_y, res_z), (rate_x, rate_y, rate_z), masks)
            ):
                if sweep > 0:
                    res = DAMPING * moment[c][x] + res
                moment[c][x] = res
                fresh[c][x] = jnp.where(mask, vel[c][x] + res * rate[x], 0.0)
        vel = fresh
    for x in range(cells_x):
        for c in range(3):
            new_vel_ref[c, x] = vel[c][x + HALO][HALO : HALO + cells_y]
        new_press_ref[x] = press[x + HALO][HALO : HALO + cells_y]
        visc_out_ref[x] = visc[x + HALO][HALO : HALO + cells_y]


def stokes(here, vel, press, buoy, visc, cells_y, sizes):
    wide_x, _, num_levels = visc.shape
    cells_x = wide_x - 2 * HALO
    return pl.pallas_call(
        functools.partial(stokes_kernel, cells_y, sizes),
        out_shape=(
            jax.ShapeDtypeStruct((3, cells_x, cells_y, num_levels), F32),
            jax.ShapeDtypeStruct((cells_x, cells_y, num_levels), F32),
            jax.ShapeDtypeStruct((cells_x, cells_y, num_levels), F32),
        ),
        in_specs=[VMEM] * 5,
        out_specs=(VMEM, VMEM, VMEM),
        compiler_params=pltpu.CompilerParams(vmem_limit_bytes=48 << 20),
        name="stokes",
    )(here, vel, press, buoy, visc)


def partners(size_x, size_y):
    def flat(x, y):
        return (x % size_x) * size_y + y

    cells = [(x, y) for x in range(size_x) for y in range(size_y)]
    x_near = [(flat(x, y), flat(x ^ 1, y)) for x, y in cells]
    x_far = [(flat(x, y), flat(x + 1 if x % 2 else x - 1, y)) for x, y in cells]
    y_near = [(flat(x, y), flat(x, y ^ 1)) for x, y in cells]
    y_far = [
        (flat(x, y), flat(x ^ 1, y) if y in (0, size_y - 1) else flat(x, y + 1 if y % 2 else y - 1))
        for x, y in cells
    ]
    return x_near, x_far, y_near, y_far


def swapped(near, far, near_pairs, far_pairs, odd, dim, x):
    near = lax.ppermute(near, ("gx", "gy"), near_pairs)
    far = lax.ppermute(far, ("gx", "gy"), far_pairs)
    before, after = jnp.where(odd, near, far), jnp.where(odd, far, near)
    return jnp.concatenate([before, x, after], axis=dim)


def strips(x, odd, dim):
    length = x.shape[dim]
    first = lax.slice_in_dim(x, 0, HALO, axis=dim)
    final = lax.slice_in_dim(x, length - HALO, length, axis=dim)
    return jnp.where(odd, first, final), jnp.where(odd, final, first)


def widened(x, near, far, pairs, odd_x, odd_y):
    dim = x.ndim - 3
    x = swapped(near, far, pairs[0], pairs[1], odd_x, dim, x)
    x = swapped(*strips(x, odd_y, dim + 1), pairs[2], pairs[3], odd_y, dim + 1, x)
    pad = jnp.zeros(x.shape[:-2] + (-x.shape[-2] % 8, x.shape[-1]), x.dtype)
    return jnp.concatenate([x, pad], axis=dim + 1)


def shards(
    velocity,
    pressure,
    buoyancy,
    background,
    marker_value,
    marker_height,
    marker_owner,
    marker_column,
    block_count,
):
    cells_x, cells_y, num_levels = pressure.shape
    block_rows, marks = marker_value.shape
    size_x = lax.axis_size("gx")
    size_y = lax.axis_size("gy")
    devices = size_x * size_y
    capacity = max(2, (2 * block_rows + devices - 1) // devices)
    send = deposit(
        block_count,
        marker_owner,
        marker_column,
        marker_value,
        marker_height,
        devices,
        capacity,
        num_levels,
    )
    arrived = lax.all_to_all(
        send.reshape(devices, capacity, 2 * num_levels),
        ("gx", "gy"),
        split_axis=0,
        concat_axis=0,
        tiled=True,
    ).reshape(devices * capacity, 2 * num_levels)
    pairs = partners(size_x, size_y)
    place_x, place_y = lax.axis_index("gx"), lax.axis_index("gy")
    odd_x, odd_y = place_x % 2, place_y % 2
    here = jnp.where(lax.broadcasted_iota(jnp.int32, (8, num_levels), 0) == 0, place_x, place_y)
    fields = jnp.concatenate([velocity, pressure[None], buoyancy[None]], axis=0)
    near, far = strips(fields, odd_x == 1, 1)
    near, here = lax.optimization_barrier((near, here))
    fields = widened(fields, near, far, pairs, odd_x == 1, odd_y == 1)
    visc, near, far = gather(here, arrived, background, marks)
    visc = widened(visc, near, far, pairs, odd_x == 1, odd_y == 1)
    return stokes(
        here, fields[:3], fields[3], fields[4], visc, cells_y, (size_x, size_y)
    )


def solution(mesh):
    return jax.shard_map(
        shards,
        mesh=mesh,
        in_specs=(
            P(None, "gx", "gy", None),
            P("gx", "gy", None),
            P("gx", "gy", None),
            P("gx", "gy", None),
            P(("gx", "gy"), None),
            P(("gx", "gy"), None),
            P(("gx", "gy"), None),
            P(("gx", "gy")),
            P(("gx", "gy")),
        ),
        out_specs=(P(None, "gx", "gy", None), P("gx", "gy", None), P("gx", "gy", None)),
        check_vma=False,
    )
```

```python
import functools

import jax
import jax.numpy as jnp
from jax import lax
from jax.experimental import pallas as pl
from jax.experimental.pallas import tpu as pltpu
from jax.sharding import PartitionSpec as P

ITERS = 2
HALO = 2
WAYS = 4
OUT_PARTS = 4

PRESS_STEP = 0.5
VEL_STEP = 0.05
DAMPING = 0.8

F32 = jnp.float32
BF16 = jnp.bfloat16
VMEM = pl.BlockSpec(memory_space=pltpu.VMEM)
HBM = pl.BlockSpec(memory_space=pltpu.HBM)
SMEM = pl.BlockSpec(memory_space=pltpu.SMEM)
NT = (((1,), (1,)), ((), ()))


def split3(x):
    high = x.astype(BF16)
    rest = x - high.astype(F32)
    mid = rest.astype(BF16)
    low = (rest - mid.astype(F32)).astype(BF16)
    return high, mid, low


def deposit_kernel(
    num_owners,
    capacity,
    count_ref,
    owner_hbm,
    column_hbm,
    value_hbm,
    height_hbm,
    out_hbm,
    value_ref,
    height_ref,
    owner_ref,
    column_ref,
    place_ref,
    code_ref,
    lower_ref,
    fraction_ref,
    part_ref,
    out_ref,
    sem,
    out_sem,
):
    blocks, marks = value_ref.shape
    num_levels = out_ref.shape[1] // 2
    slots = num_owners * capacity

    copies = (
        pltpu.make_async_copy(owner_hbm, owner_ref, sem.at[0]),
        pltpu.make_async_copy(column_hbm, column_ref, sem.at[1]),
        pltpu.make_async_copy(height_hbm, height_ref, sem.at[2]),
        pltpu.make_async_copy(value_hbm, value_ref, sem.at[3]),
    )
    for copy in copies:
        copy.start()
    for copy in copies:
        copy.wait()

    owner = owner_ref[...]
    block_id = lax.broadcasted_iota(jnp.int32, (1, blocks), 1)
    owner = jnp.where(block_id < count_ref[0], owner, num_owners)
    owned = lax.broadcasted_iota(jnp.int32, (num_owners, blocks), 0) == owner
    hits = jnp.where(owned, 1.0, 0.0)
    earlier = jnp.where(
        lax.broadcasted_iota(jnp.int32, (blocks, blocks), 0)
        < lax.broadcasted_iota(jnp.int32, (blocks, blocks), 1),
        1.0,
        0.0,
    ).astype(BF16)
    before = jnp.dot(hits.astype(BF16), earlier, preferred_element_type=F32)
    rank = jnp.sum(hits * before, axis=0, keepdims=True)
    slot = owner * capacity + rank.astype(jnp.int32)
    place = jnp.where(
        lax.broadcasted_iota(jnp.int32, (slots, blocks), 0) == slot, 1.0, 0.0
    ).astype(BF16)
    place_ref[...] = place
    code = jnp.broadcast_to((column_ref[...] + 1).astype(F32), (num_levels, blocks)).astype(BF16)
    code_ref[...] = lax.dot_general(place, code, NT, preferred_element_type=F32)

    span = num_levels // WAYS
    row8 = lax.broadcasted_iota(jnp.int32, (8, marks), 0)
    upper_part = (row8 & 1) == 1
    with_value = (row8 & 2) == 0
    leading = row8 < 4
    offset_id = lax.broadcasted_iota(jnp.int32, (span, marks), 0).astype(F32).astype(BF16)
    lane_window = lax.broadcasted_iota(jnp.int32, (8, num_levels), 1) // span

    def operands(b):
        lower = jnp.broadcast_to(lower_ref[pl.ds(b, 1), :], (8, marks))
        fraction = jnp.broadcast_to(fraction_ref[pl.ds(b, 1), :], (8, marks))
        value = jnp.broadcast_to(value_ref[pl.ds(b, 1), :], (8, marks))
        share = jnp.where(upper_part, fraction, 1.0 - fraction)
        share = share * jnp.where(with_value, value, 1.0)
        high = share.astype(BF16).astype(F32)
        pieces = jnp.where(leading, high, share - high)
        window = jnp.floor(lower * (1.0 / span))
        offset = lower - window * span
        offset = jnp.concatenate([offset, offset], axis=0).astype(BF16)
        offset = jnp.concatenate([offset] * (span // 16), axis=0)
        hot = jnp.where(offset == offset_id, jnp.ones((), BF16), jnp.zeros((), BF16))
        return [jnp.where(window == a, pieces, 0.0) for a in range(WAYS)], hot

    height = height_ref[...]
    lower = jnp.minimum(jnp.floor(height), num_levels - 2.0)
    lower_ref[...] = lower
    fraction_ref[...] = height - lower
    for b in range(0, blocks, WAYS):
        pieces, hots = zip(*(operands(b + i) for i in range(WAYS)))
        sums = lax.dot_general(
            jnp.concatenate(sum(pieces, []), axis=0).astype(BF16),
            jnp.concatenate(hots, axis=0),
            NT,
            preferred_element_type=F32,
        )
        for i in range(WAYS):
            total = jnp.zeros((8, num_levels), F32)
            for a in range(WAYS):
                found = sums[(i * WAYS + a) * 8 : (i * WAYS + a + 1) * 8]
                turn = ((a - i) * span) % num_levels
                found = pltpu.roll(found, turn, 1) if turn else found
                total = jnp.where(lane_window == a, found, total)
            part_ref[(b + i) * 8 : (b + i + 1) * 8, :] = total

    def part(kind):
        high = part_ref[pl.ds(kind, blocks, stride=8), :]
        return high + part_ref[pl.ds(kind + 4, blocks, stride=8), :]

    value_sum = part(0) + pltpu.roll(part(1), 1, 1)
    weight_sum = part(2) + pltpu.roll(part(3), 1, 1)
    pieces = split3(jnp.concatenate([value_sum, weight_sum], axis=1))
    size = slots // OUT_PARTS
    copies = []
    for p in range(OUT_PARTS):
        rows = slice(p * size, (p + 1) * size)
        high, mid, low = (
            jnp.dot(place_ref[rows], y, preferred_element_type=F32) for y in pieces
        )
        sums = high + (mid + low)
        lane = lax.broadcasted_iota(jnp.int32, (size, num_levels), 1)
        out_ref[rows, :num_levels] = sums[:, :num_levels]
        out_ref[rows, num_levels:] = jnp.where(
            lane == num_levels - 1, code_ref[rows], sums[:, num_levels:]
        )
        copy = pltpu.make_async_copy(out_ref.at[rows], out_hbm.at[rows], out_sem.at[p])
        copy.start()
        copies.append(copy)
    for copy in copies:
        copy.wait()


def deposit(count, owner, column, value, height, num_owners, capacity, num_levels):
    blocks, marks = value.shape
    slots = num_owners * capacity
    return pl.pallas_call(
        functools.partial(deposit_kernel, num_owners, capacity),
        out_shape=jax.ShapeDtypeStruct((slots, 2 * num_levels), F32),
        in_specs=[SMEM, HBM, HBM, HBM, HBM],
        out_specs=HBM,
        scratch_shapes=[
            pltpu.VMEM((blocks, marks), F32),
            pltpu.VMEM((blocks, marks), F32),
            pltpu.VMEM((1, blocks), jnp.int32),
            pltpu.VMEM((1, blocks), jnp.int32),
            pltpu.VMEM((slots, blocks), BF16),
            pltpu.VMEM((slots, num_levels), F32),
            pltpu.VMEM((blocks, marks), F32),
            pltpu.VMEM((blocks, marks), F32),
            pltpu.VMEM((blocks * 8 + 8, num_levels), F32),
            pltpu.VMEM((slots, 2 * num_levels), F32),
            pltpu.SemaphoreType.DMA((4,)),
            pltpu.SemaphoreType.DMA((OUT_PARTS,)),
        ],
        compiler_params=pltpu.CompilerParams(vmem_limit_bytes=60 << 20),
        name="deposit",
    )(count, owner.reshape(1, blocks), column.reshape(1, blocks), value, height)


def gather_kernel(marks, here_ref, arrived_ref, background_ref, out_ref, near_ref, far_ref):
    slots = arrived_ref.shape[0]
    cells_x, cells_y, num_levels = out_ref.shape
    columns = cells_x * cells_y
    values = arrived_ref[:, :num_levels]
    weights = arrived_ref[:, num_levels:]
    last = lax.broadcasted_iota(jnp.int32, (slots, num_levels), 1) == num_levels - 1
    pick = jnp.where(
        lax.broadcasted_iota(jnp.int32, (8, num_levels), 1) == num_levels - 1, 1.0, 0.0
    ).astype(BF16)
    column_id = (lax.broadcasted_iota(jnp.int32, (columns, slots), 0) + 1).astype(F32)
    codes = lax.dot_general(pick, weights.astype(BF16), NT, preferred_element_type=F32)
    place = jnp.where(codes[:1] == column_id, 1.0, 0.0).astype(BF16)
    others = jnp.sum(jnp.where(last, 0.0, weights), axis=1, keepdims=True)
    weights = jnp.where(last, float(marks) - others, weights)
    high, mid, low = (
        jnp.dot(place, y, preferred_element_type=F32)
        for y in split3(jnp.concatenate([values, weights], axis=1))
    )
    sums = high + (mid + low)
    background = background_ref[...].reshape(columns, num_levels)
    visc = jnp.exp((sums[:, :num_levels] + background) / (sums[:, num_levels:] + 1.0))
    visc = visc.reshape(cells_x, cells_y, num_levels)
    out_ref[...] = visc
    odd = here_ref[:1, :] % 2 == 1
    first, final = visc[:HALO], visc[cells_x - HALO :]
    near_ref[...] = jnp.where(odd, first, final)
    far_ref[...] = jnp.where(odd, final, first)


def gather(here, arrived, background, marks):
    strip = (HALO,) + background.shape[1:]
    return pl.pallas_call(
        functools.partial(gather_kernel, marks),
        out_shape=(
            jax.ShapeDtypeStruct(background.shape, F32),
            jax.ShapeDtypeStruct(strip, F32),
            jax.ShapeDtypeStruct(strip, F32),
        ),
        in_specs=[VMEM, VMEM, VMEM],
        out_specs=(VMEM, VMEM, VMEM),
        compiler_params=pltpu.CompilerParams(vmem_limit_bytes=48 << 20),
        name="gather",
    )(here, arrived, background)


def stokes_kernel(
    cells_y,
    sizes,
    here_ref,
    vel_ref,
    press_ref,
    buoy_ref,
    own_ref,
    west_ref,
    east_ref,
    near_ref,
    far_ref,
    new_vel_ref,
    new_press_ref,
    visc_out_ref,
    visc_ref,
):
    wide_x, rows, num_levels = visc_ref.shape
    cells_x = wide_x - 2 * HALO
    inner, end = slice(HALO, HALO + cells_y), HALO + cells_y
    odd_y = here_ref[1:2, :] % 2 == 1
    near, far = near_ref[...], far_ref[...]
    visc_ref[:HALO, inner] = west_ref[...]
    visc_ref[HALO : HALO + cells_x, inner] = own_ref[...]
    visc_ref[HALO + cells_x :, inner] = east_ref[...]
    visc_ref[:, :HALO] = jnp.where(odd_y, near, far)
    visc_ref[:, end : end + HALO] = jnp.where(odd_y, far, near)
    visc_ref[:, end + HALO :] = jnp.zeros((wide_x, rows - end - HALO, num_levels), F32)
    row = lax.broadcasted_iota(jnp.int32, (rows, num_levels), 0)
    lane = lax.broadcasted_iota(jnp.int32, (rows, num_levels), 1)
    size_x, size_y = sizes[0] * cells_x, sizes[1] * cells_y
    first_x = jnp.broadcast_to(here_ref[:1, :], row.shape) * cells_x
    at_y = row + (here_ref[1:2, :] * cells_y - HALO)
    in_y = (at_y >= 0) & (at_y < size_y)
    in_y_face = (at_y >= 0) & (at_y < size_y - 1)
    low_lane = lane == 0
    high_lane = lane == num_levels - 1

    def north(f):
        return pltpu.roll(f, rows - 1, 0)

    def south(f):
        return pltpu.roll(f, 1, 0)

    def upper(f):
        return jnp.where(high_lane, 0.0, pltpu.roll(f, num_levels - 1, 1))

    def lower(f):
        return jnp.where(low_lane, 0.0, pltpu.roll(f, 1, 1))

    def in_x(x):
        at_x = first_x - HALO + x
        return (at_x >= 0) & (at_x < size_x)

    def in_x_face(x):
        at_x = first_x - HALO + x
        return (at_x >= 0) & (at_x < size_x - 1)

    inside = [in_y & in_x(x) for x in range(wide_x)]

    def known(ref, x, *lead):
        return jnp.where(inside[x], ref[(*lead, x)], 0.0)

    visc = [known(visc_ref, x) for x in range(wide_x)]
    vel = [[known(vel_ref, x, c) for x in range(wide_x)] for c in range(3)]
    press = [known(press_ref, x) for x in range(wide_x)]
    side_x = [visc[x] + visc[x + 1] for x in range(wide_x - 1)]
    side_y = [visc[x] + north(visc[x]) for x in range(wide_x)]
    side_z = [visc[x] + upper(visc[x]) for x in range(wide_x)]
    corner_xy = [0.25 * (side_y[x] + side_y[x + 1]) for x in range(wide_x - 1)]
    corner_xz = [0.25 * (side_x[x] + upper(side_x[x])) for x in range(wide_x - 1)]
    corner_yz = [0.25 * (side_y[x] + upper(side_y[x])) for x in range(wide_x)]
    rate_x = [(2.0 * VEL_STEP) / side for side in side_x]
    rate_y = [(2.0 * VEL_STEP) / side for side in side_y]
    rate_z = [(2.0 * VEL_STEP) / side for side in side_z]
    moment = [[None] * wide_x for _ in range(3)]
    for sweep in range(ITERS):
        begin, end = sweep, wide_x - sweep
        sig_x, sig_y, sig_z = {}, {}, {}
        tau_xy, tau_xz, tau_yz = {}, {}, {}
        for x in range(begin, end):
            u, v, w = vel[0][x], vel[1][x], vel[2][x]
            if x > begin:
                grad_x = u - vel[0][x - 1]
                grad_y = v - south(v)
                grad_z = w - lower(w)
                div = grad_x + grad_y + grad_z
                press[x] = press[x] - PRESS_STEP * visc[x] * div
                third = div / 3.0
                twice = 2.0 * visc[x]
                sig_x[x] = twice * (grad_x - third) - press[x]
                sig_y[x] = twice * (grad_y - third) - press[x]
                sig_z[x] = twice * (grad_z - third) - press[x]
                tau_yz[x] = jnp.where(
                    in_y, corner_yz[x] * (upper(v) - v + north(w) - w), 0.0
                )
            if x < end - 1:
                tau_xy[x] = jnp.where(
                    inside[x], corner_xy[x] * (north(u) - u + vel[1][x + 1] - v), 0.0
                )
                tau_xz[x] = jnp.where(
                    in_x(x), corner_xz[x] * (upper(u) - u + vel[2][x + 1] - w), 0.0
                )
        fresh = [[None] * wide_x for _ in range(3)]
        for x in range(begin + 1, end - 1):
            res_x = (
                sig_x[x + 1]
                - sig_x[x]
                + tau_xy[x]
                - south(tau_xy[x])
                + tau_xz[x]
                - lower(tau_xz[x])
            )
            res_y = (
                tau_xy[x]
                - tau_xy[x - 1]
                + north(sig_y[x])
                - sig_y[x]
                + tau_yz[x]
                - lower(tau_yz[x])
            )
            res_z = (
                tau_xz[x]
                - tau_xz[x - 1]
                + tau_yz[x]
                - south(tau_yz[x])
                + upper(sig_z[x])
                - sig_z[x]
                + buoy_ref[x]
            )
            masks = (
                in_y & in_x_face(x),
                in_y_face & in_x(x),
                (in_y & jnp.logical_not(high_lane)) & in_x(x),
            )
            for c, (res, rate, mask) in enumerate(
                zip((res_x, res_y, res_z), (rate_x, rate_y, rate_z), masks)
            ):
                if sweep > 0:
                    res = DAMPING * moment[c][x] + res
                moment[c][x] = res
                fresh[c][x] = jnp.where(mask, vel[c][x] + res * rate[x], 0.0)
        vel = fresh
    for x in range(cells_x):
        for c in range(3):
            new_vel_ref[c, x] = vel[c][x + HALO][HALO : HALO + cells_y]
        new_press_ref[x] = press[x + HALO][HALO : HALO + cells_y]
        visc_out_ref[x] = visc[x + HALO][HALO : HALO + cells_y]


def stokes(here, vel, press, buoy, visc, cells_y, sizes):
    wide_x, _, num_levels = press.shape
    cells_x = wide_x - 2 * HALO
    return pl.pallas_call(
        functools.partial(stokes_kernel, cells_y, sizes),
        out_shape=(
            jax.ShapeDtypeStruct((3, cells_x, cells_y, num_levels), F32),
            jax.ShapeDtypeStruct((cells_x, cells_y, num_levels), F32),
            jax.ShapeDtypeStruct((cells_x, cells_y, num_levels), F32),
        ),
        in_specs=[VMEM] * 9,
        out_specs=(VMEM, VMEM, VMEM),
        scratch_shapes=[pltpu.VMEM(press.shape, F32)],
        compiler_params=pltpu.CompilerParams(vmem_limit_bytes=48 << 20),
        name="stokes",
    )(here, vel, press, buoy, *visc)


def partners(size_x, size_y):
    def flat(x, y):
        return (x % size_x) * size_y + y

    cells = [(x, y) for x in range(size_x) for y in range(size_y)]
    x_near = [(flat(x, y), flat(x ^ 1, y)) for x, y in cells]
    x_far = [(flat(x, y), flat(x + 1 if x % 2 else x - 1, y)) for x, y in cells]
    y_near = [(flat(x, y), flat(x, y ^ 1)) for x, y in cells]
    y_far = [
        (flat(x, y), flat(x ^ 1, y) if y in (0, size_y - 1) else flat(x, y + 1 if y % 2 else y - 1))
        for x, y in cells
    ]
    return x_near, x_far, y_near, y_far


def swapped(near, far, near_pairs, far_pairs, odd, dim, x):
    near = lax.ppermute(near, ("gx", "gy"), near_pairs)
    far = lax.ppermute(far, ("gx", "gy"), far_pairs)
    before, after = jnp.where(odd, near, far), jnp.where(odd, far, near)
    return jnp.concatenate([before, x, after], axis=dim)


def strips(x, odd, dim):
    length = x.shape[dim]
    first = lax.slice_in_dim(x, 0, HALO, axis=dim)
    final = lax.slice_in_dim(x, length - HALO, length, axis=dim)
    return jnp.where(odd, first, final), jnp.where(odd, final, first)


def widened(x, near, far, pairs, odd_x, odd_y):
    dim = x.ndim - 3
    x = swapped(near, far, pairs[0], pairs[1], odd_x, dim, x)
    x = swapped(*strips(x, odd_y, dim + 1), pairs[2], pairs[3], odd_y, dim + 1, x)
    pad = jnp.zeros(x.shape[:-2] + (-x.shape[-2] % 8, x.shape[-1]), x.dtype)
    return jnp.concatenate([x, pad], axis=dim + 1)


def shards(
    velocity,
    pressure,
    buoyancy,
    background,
    marker_value,
    marker_height,
    marker_owner,
    marker_column,
    block_count,
):
    cells_x, cells_y, num_levels = pressure.shape
    block_rows, marks = marker_value.shape
    size_x = lax.axis_size("gx")
    size_y = lax.axis_size("gy")
    devices = size_x * size_y
    capacity = max(2, (2 * block_rows + devices - 1) // devices)
    send = deposit(
        block_count,
        marker_owner,
        marker_column,
        marker_value,
        marker_height,
        devices,
        capacity,
        num_levels,
    )
    arrived = lax.all_to_all(
        send.reshape(devices, capacity, 2 * num_levels),
        ("gx", "gy"),
        split_axis=0,
        concat_axis=0,
        tiled=True,
    ).reshape(devices * capacity, 2 * num_levels)
    pairs = partners(size_x, size_y)
    place_x, place_y = lax.axis_index("gx"), lax.axis_index("gy")
    odd_x, odd_y = place_x % 2, place_y % 2
    here = jnp.where(lax.broadcasted_iota(jnp.int32, (8, num_levels), 0) == 0, place_x, place_y)
    fields = jnp.concatenate([velocity, pressure[None], buoyancy[None]], axis=0)
    near, far = strips(fields, odd_x == 1, 1)
    near, here = lax.optimization_barrier((near, here))
    fields = widened(fields, near, far, pairs, odd_x == 1, odd_y == 1)
    visc, near, far = gather(here, arrived, background, marks)
    wide = swapped(near, far, pairs[0], pairs[1], odd_x == 1, 0, visc)
    near, far = strips(wide, odd_y == 1, 1)
    near = lax.ppermute(near, ("gx", "gy"), pairs[2])
    far = lax.ppermute(far, ("gx", "gy"), pairs[3])
    visc = (visc, wide[:HALO], wide[HALO + cells_x :], near, far)
    return stokes(
        here, fields[:3], fields[3], fields[4], visc, cells_y, (size_x, size_y)
    )


def solution(mesh):
    return jax.shard_map(
        shards,
        mesh=mesh,
        in_specs=(
            P(None, "gx", "gy", None),
            P("gx", "gy", None),
            P("gx", "gy", None),
            P("gx", "gy", None),
            P(("gx", "gy"), None),
            P(("gx", "gy"), None),
            P(("gx", "gy"), None),
            P(("gx", "gy")),
            P(("gx", "gy")),
        ),
        out_specs=(P(None, "gx", "gy", None), P("gx", "gy", None), P("gx", "gy", None)),
        check_vma=False,
    )
```
